128 devices in a mesh: gx: 2 (over core), gy: 64 (over z, y, x).
Axes of the slice: x: 4, y: 4, z: 4, core: 2. Of those that a mesh axis runs over, the one named last changes fastest.
Arguments:
- velocity: float32 [2, 32, 256, 8192], P(None, None, 'gx', 'gy'), may hold values from -2.5 to 2.5
- stream_metric: float32 [256], replicated, may hold values from 0.5 to 2
- wall_metric: float32 [8192], replicated, may hold values from 0.5 to 2
Outputs:
- advection: float32 [3, 32, 256, 8192], P(None, None, 'gx', 'gy')
The draws below stay inside these ranges and needn't reach their ends.
All inputs are finite; a program needn't handle non-finite values.
Results may differ from the reference program's by a relative error of at most 0.0003.
Values sent between devices are 32-bit elements; how exact they have to be, the bound alone decides.
A program may use at most 256 MiB of HBM per device.

```python
import math
import jax
import jax.numpy as jnp
from jax import lax

NZ = 32
NX = 256
NY = 8192


def steps_of(rng, shape, shards, least, high):
    loudness, own = 1.0, jax.random.fold_in(rng, 6)
    for position, shards_of in shards:
        draws = jnp.exp(jax.random.uniform(jax.random.fold_in(own, position), (shards_of,), jnp.float32, least / len(shards), high / len(shards)))
        loudness = loudness * jnp.repeat(draws, shape[position] // shards_of).reshape([-1 if axis == position else 1 for axis in range(len(shape))])
    return loudness


def normal_values(rng, shape, spread, most, cuts=(), kind=jnp.bfloat16):
    factor_of = steps_of(rng, shape, cuts, -0.22, 0.18) if cuts else 1.0
    values = jax.random.normal(rng, shape, jnp.float32) * spread * factor_of
    return jnp.minimum(jnp.maximum(values, -most), most).astype(kind)


def setup_inputs(seed: int = 0) -> dict:
    keys = jax.random.split(jax.random.key(seed), 4)
    return {
        "velocity": normal_values(keys[0], (2, NZ, NX, NY), 0.25, 2.5, ((2, 2), (3, 64)), jnp.float32),
        "stream_metric": jnp.clip(jnp.exp(jax.random.uniform(keys[1], (NX,), jnp.float32, math.log(0.5), math.log(2.0))), 0.5, 2.0),
        "wall_metric": jnp.clip(jnp.exp(jax.random.uniform(keys[2], (NY,), jnp.float32, math.log(0.5), math.log(2.0))), 0.5, 2.0),
    }


CENTRAL = (0.75, -0.15, 1.0 / 60.0)


def periodic_slope(values, dimension):
    result = jnp.zeros_like(values)
    for distance, weight in enumerate(CENTRAL, start=1):
        result = result + weight * (jnp.roll(values, -distance, axis=dimension) - jnp.roll(values, distance, axis=dimension))
    return result


def wall_slope(values):
    rows_all = values.shape[-1]
    pad_width = [(0, 0)] * (values.ndim - 1) + [(3, 3)]
    padded = jnp.pad(values, pad_width)

    def shifted(offset):
        return padded[..., 3 + offset:3 + offset + rows_all]

    result = jnp.zeros_like(values)
    for distance, weight in enumerate(CENTRAL, start=1):
        result = result + weight * (shifted(distance) - shifted(-distance))
    first_row = (-11.0 * values[..., 0] + 18.0 * values[..., 1] - 9.0 * values[..., 2] + 2.0 * values[..., 3]) / 6.0
    second_row = (-2.0 * values[..., 0] - 3.0 * values[..., 1] + 6.0 * values[..., 2] - values[..., 3]) / 6.0
    third_row = (8.0 * (values[..., 3] - values[..., 1]) - (values[..., 4] - values[..., 0])) / 12.0
    third_last = (8.0 * (values[..., -2] - values[..., -4]) - (values[..., -1] - values[..., -5])) / 12.0
    second_last = (2.0 * values[..., -1] + 3.0 * values[..., -2] - 6.0 * values[..., -3] + values[..., -4]) / 6.0
    last_row = (11.0 * values[..., -1] - 18.0 * values[..., -2] + 9.0 * values[..., -3] - 2.0 * values[..., -4]) / 6.0
    result = result.at[..., 0].set(first_row)
    result = result.at[..., 1].set(second_row)
    result = result.at[..., 2].set(third_row)
    result = result.at[..., -3].set(third_last)
    result = result.at[..., -2].set(second_last)
    result = result.at[..., -1].set(last_row)
    return result


def reference(velocity, stream_metric, wall_metric):
    streamwise = velocity[0]
    spanwise = velocity[1]
    stream_scale = stream_metric[None, :, None]
    wall_scale = wall_metric[None, None, :]
    divergence = stream_scale * periodic_slope(streamwise, 1) + periodic_slope(spanwise, 0)
    slope = divergence / wall_scale
    cell_height = 1.0 / wall_metric
    height = jnp.cumsum(cell_height) - 0.5 * cell_height
    total_height = jnp.sum(cell_height)
    rise = jnp.cumsum(slope, axis=2) - 0.5 * slope
    rise_total = jnp.sum(slope, axis=2)
    normal = -(rise - (height / total_height)[None, None, :] * rise_total[:, :, None])
    fields = jnp.stack([streamwise, normal, spanwise])
    offsets = jnp.arange(-3, 4, dtype=jnp.int32)
    stream_plane = stream_metric[None, :, None]
    wall_plane = wall_metric[None, None, :]

    def one_plane(plane_index, output):
        indices = (plane_index + offsets).astype(jnp.int32) % NZ
        planes = jnp.take(fields, indices, axis=1)
        span_products = planes[2:3] * planes
        span_slopes = jnp.zeros_like(planes[:, 3])
        span_fluxes = jnp.zeros_like(planes[:, 3])
        for distance, weight in enumerate(CENTRAL, start=1):
            span_slopes = span_slopes + weight * (planes[:, 3 + distance] - planes[:, 3 - distance])
            span_fluxes = span_fluxes + weight * (span_products[:, 3 + distance] - span_products[:, 3 - distance])
        middle = planes[:, 3]
        stream_slopes = periodic_slope(middle, 1) * stream_plane
        stream_fluxes = periodic_slope(middle[0:1] * middle, 1) * stream_plane
        wall_slopes = wall_slope(middle) * wall_plane
        wall_fluxes = wall_slope(middle[1:2] * middle) * wall_plane
        advection = 0.5 * (middle[0] * stream_slopes + middle[1] * wall_slopes + middle[2] * span_slopes + stream_fluxes + wall_fluxes + span_fluxes)
        return lax.dynamic_update_index_in_dim(output, advection, plane_index, axis=1)

    initial = jnp.zeros((3,) + velocity.shape[1:], jnp.float32)
    return lax.fori_loop(0, NZ, one_plane, initial)
```

```python
import functools

import jax
import jax.numpy as jnp
from jax import lax
from jax.experimental import pallas as pl
from jax.experimental.pallas import tpu as pltpu
from jax.sharding import PartitionSpec as P

MESH = pl.DeviceIdType.MESH
F32 = jnp.float32
L = 128
HALO = 8
EDGE = 4
WIDE = L + 2 * HALO
SPAN = L + 2 * EDGE
CENTRAL = (45.0, -9.0, 1.0)
INTERIOR = (-1.0 / 60.0, 0.15, -0.75, 0.0, 0.75, -0.15, 1.0 / 60.0)
ROW_FIRST = (0.0, 0.0, 0.0, -11.0 / 6.0, 3.0, -1.5, 1.0 / 3.0)
ROW_SECOND = (0.0, 0.0, -1.0 / 3.0, -0.5, 1.0, -1.0 / 6.0, 0.0)
ROW_THIRD = (0.0, 1.0 / 12.0, -2.0 / 3.0, 0.0, 2.0 / 3.0, -1.0 / 12.0, 0.0)
ROW_SECOND_LAST = (0.0, 1.0 / 6.0, -1.0, 0.5, 1.0 / 3.0, 0.0, 0.0)
ROW_LAST = (-1.0 / 3.0, 1.5, -3.0, 11.0 / 6.0, 0.0, 0.0, 0.0)
TILES = SPAN // 8
GROUPS = -(-TILES // 4)
ROW_FRAC, ROW_SLOTS, ROW_EDGES = 7, 8, 12
ROWS = 18
FRONT, BACK, NEXT, PREV = range(4)


def rings_of(count):
    size = 4 if count % 4 == 0 and count > 16 else 2
    rings, stride = [], 1
    while stride < count:
        rings.append((stride, size))
        stride *= size
    return rings


def lanes(shape):
    return lax.broadcasted_iota(jnp.int32, shape, len(shape) - 1)


def rolled(x, shift):
    if isinstance(shift, int):
        shift %= L
        if shift == 0:
            return x
    return pltpu.roll(x, shift, len(x.shape) - 1)


def running(x):
    lane = lanes(x.shape)
    step = 1
    while step < L:
        x = x + jnp.where(lane >= step, rolled(x, step), 0.0)
        step *= 2
    return x


def scaled(x, weight):
    return x if weight == 1.0 else x * weight


def chunks(total, size):
    return [(i, min(size, total - i)) for i in range(0, total, size)]


def skew(adv, fields):
    centre = adv(0)
    sums = [None] * len(fields)
    for d, weight in enumerate(CENTRAL, start=1):
        up = scaled(centre + adv(d), weight)
        down = scaled(centre + adv(-d), weight)
        for n, field in enumerate(fields):
            term = up * field(d) - down * field(-d)
            sums[n] = term if sums[n] is None else sums[n] + term
    return sums


def slope_sum(field):
    total = None
    for d, weight in enumerate(CENTRAL, start=1):
        term = scaled(field(d) - field(-d), weight)
        total = term if total is None else total + term
    return total


def first_kernel(
    n_gy, depth,
    vel, sm, wm,
    uw, crow, halo, chalo, part, below_total, rows, m120,
    slope, m_wide, pack, spack, sland, stage_out, stage_in, tot_pack,
    load_sem, gx_send, gx_recv, y_send, y_recv, st_send, st_recv,
):
    gx, gy = lax.axis_index("gx"), lax.axis_index("gy")
    other = 1 - gx
    rings = rings_of(n_gy)
    up_gy, down_gy = lax.rem(gy + 1, n_gy), lax.rem(gy + n_gy - 1, n_gy)

    def peer(stride, size, offset):
        place = lax.rem(gy // stride, size)
        return gy + (lax.rem(place + offset, size) - place) * stride

    half = depth // 2
    loads = []
    for f in range(2):
        for h in range(2):
            loads.append(pltpu.make_async_copy(
                vel.at[f, pl.ds(h * half, half)],
                uw.at[f, pl.ds(h * half, half), pl.ds(HALO, L)],
                load_sem.at[f, h]))
            loads[-1].start()

    barrier = pltpu.get_barrier_semaphore()
    count = 0
    targets = [{"gx": other}, {"gy": up_gy}, {"gy": down_gy}]
    for stride, size in rings:
        targets += [{"gy": peer(stride, size, o)} for o in range(1, size)]
    for target in targets:
        pl.semaphore_signal(barrier, inc=1, device_id=target, device_id_type=MESH)
        count += 1

    rid = lax.broadcasted_iota(jnp.int32, (n_gy, L), 0)
    wall = wm[...]
    recip = 1.0 / wall

    def row_at(values, index):
        picked = jnp.sum(jnp.where(rid == index, values, 0.0), axis=0, keepdims=True)
        return jnp.broadcast_to(picked, (8, L))

    def whole(values):
        return jnp.sum(jnp.sum(values, axis=0, keepdims=True), axis=1, keepdims=True)

    total_h = whole(recip)
    below_h = whole(jnp.where(rid < gy, recip, 0.0))
    r_own, r_next, r_prev = row_at(recip, gy), row_at(recip, up_gy), row_at(recip, down_gy)
    wall_own = row_at(wall, gy)
    lane8 = lanes((8, L))
    run_own, run_next, run_prev = running(r_own), running(r_next), running(r_prev)
    sum_own = jnp.sum(r_own[0:1], axis=1, keepdims=True)
    sum_prev = jnp.sum(r_prev[0:1], axis=1, keepdims=True)
    frac = (below_h + (run_own - 0.5 * r_own)) / total_h
    frac_next = (below_h + sum_own + (run_next - 0.5 * r_next)) / total_h
    frac_prev = (below_h - sum_prev + (run_prev - 0.5 * r_prev)) / total_h
    rows[ROW_FRAC] = frac

    def slots(values, start):
        values = jnp.where(lane8 < 4, rolled(values, -start), 0.0)
        step = 4
        while step < L:
            values = values + rolled(values, step)
            step *= 2
        return values

    for n, (values, start) in enumerate(((frac, 0), (frac, L - 4), (frac_next, 0), (frac_prev, L - 4))):
        rows[ROW_SLOTS + n] = slots(values, start)
    place = gy * L + lane8
    last = n_gy * L
    within8 = lax.rem(lane8, 4)
    for k in range(7):
        entry = jnp.full((8, L), INTERIOR[k], F32)
        for row, table in ((0, ROW_FIRST), (1, ROW_SECOND), (2, ROW_THIRD), (last - 3, ROW_THIRD),
                           (last - 2, ROW_SECOND_LAST), (last - 1, ROW_LAST)):
            entry = jnp.where(place == row, table[k], entry)
        entry = entry * (0.5 * wall_own)
        reach = lane8 + (k - 3)
        rows[k] = jnp.where((reach >= 0) & (reach < L), entry, 0.0)
        d = k - 3
        if d > 0:
            rows[ROW_EDGES + d - 1] = jnp.where(within8 + d >= 4, slots(entry, L - 4), 0.0)
        if d < 0:
            rows[ROW_EDGES + 2 - d] = jnp.where(within8 + d < 0, slots(entry, 0), 0.0)
    r60 = r_own[0:1] * (1.0 / 60.0)

    first_row, second_row = sm[0:1, :], sm[1:2, :]
    own_m = jnp.where(gx == 0, first_row, second_row)
    other_m = jnp.where(gx == 0, second_row, first_row)
    own_cols = jnp.broadcast_to(own_m, (L, L)).T
    other_cols = jnp.broadcast_to(other_m, (L, L)).T
    m_wide[0:HALO, :] = other_cols[L - HALO:L, :]
    m_wide[HALO:HALO + L, :] = own_cols
    m_wide[HALO + L:WIDE, :] = other_cols[0:HALO, :]
    m120[...] = own_cols * (1.0 / 120.0)

    pl.semaphore_wait(barrier, count)

    gx_copies = []
    for f in range(2):
        for side, (src, dst) in enumerate(((L - HALO, 0), (0, HALO + L))):
            gx_copies.append(pltpu.make_async_remote_copy(
                src_ref=vel.at[f, :, pl.ds(src, HALO)], dst_ref=uw.at[f, :, pl.ds(dst, HALO)],
                send_sem=gx_send.at[f, side], recv_sem=gx_recv.at[f, side],
                device_id={"gx": other}, device_id_type=MESH))
            gx_copies[-1].start()

    for copy in loads:
        copy.wait()

    def pack_field(read, out, extent):
        for x0, size in chunks(extent, 32):
            slot = lanes((size, L)) // 4

            def body(z, carry):
                front, back = carry
                value = read(z, x0, size)
                mine = slot == z
                front = jnp.where(mine, pltpu.roll(value, 4 * z, 1), front)
                back = jnp.where(mine, pltpu.roll(value, lax.rem(4 * z + 4, L), 1), back)
                return front, back

            zero = jnp.zeros((size, L), F32)
            front, back = lax.fori_loop(0, depth, body, (zero, zero))
            out(0, x0, size, front)
            out(1, x0, size, back)

    for f in range(2):
        def store(side, x0, size, value, f=f):
            pack[side, f, pl.ds(x0, size), :] = value

        pack_field(lambda z, x0, size, f=f: uw[f, z, pl.ds(HALO + x0, size), :], store, L)

    y_copies = []
    for side, target in ((0, down_gy), (1, up_gy)):
        y_copies.append(pltpu.make_async_remote_copy(
            src_ref=pack.at[side], dst_ref=halo.at[side],
            send_sem=y_send.at[0, side], recv_sem=y_recv.at[0, side],
            device_id={"gy": target}, device_id_type=MESH))
        y_copies[-1].start()

    for copy in gx_copies:
        copy.wait()

    lane_small = lanes((8, L))
    shift = HALO - EDGE

    def around(z, d):
        return lax.rem(z + (depth + d), depth)

    def slope_plane(z, sums):
        sums = list(sums)
        for x0, size in chunks(SPAN, 32):
            du = slope_sum(lambda d: uw[0, z, pl.ds(shift + x0 + d, size), :])
            dw = slope_sum(lambda d: uw[1, around(z, d), pl.ds(shift + x0, size), :])
            value = (m_wide[pl.ds(shift + x0, size), :] * du + dw) * r60
            slope[z, pl.ds(x0, size), :] = value
            line = jnp.sum(value, axis=1, keepdims=True)
            for t in range(size // 8):
                tile = x0 // 8 + t
                group, quarter = tile // 4, tile % 4
                sums[group] = jnp.where(lane_small == 32 * quarter + z, line[8 * t:8 * t + 8], sums[group])
        return tuple(sums)

    sums = lax.fori_loop(0, depth, slope_plane, tuple(jnp.zeros((8, L), F32) for _ in range(GROUPS)))
    own = jnp.concatenate(sums, axis=0)

    def send_stage(stage):
        stride, size = rings[stage]
        copies = []
        for o in range(1, size):
            copies.append(pltpu.make_async_remote_copy(
                src_ref=stage_out.at[stage], dst_ref=stage_in.at[stage, o - 1],
                send_sem=st_send.at[stage, o - 1], recv_sem=st_recv.at[stage, o - 1],
                device_id={"gy": peer(stride, size, o)}, device_id_type=MESH))
            copies[-1].start()
        return copies

    def plane_terms(z, carry):
        for x0, size in chunks(L, 32):
            def at(f):
                return lambda d: uw[f, z, pl.ds(HALO + x0 + d, size), :]

            def over(f):
                return lambda d: uw[f, around(z, d), pl.ds(HALO + x0, size), :]

            along_x = skew(at(0), (at(0), at(1)))
            along_z = skew(over(1), (over(0), over(1)))
            m = m120[pl.ds(x0, size), :]
            for f in range(2):
                part[f, z, pl.ds(x0, size), :] = m * along_x[f] + along_z[f] * (1.0 / 120.0)
        return carry

    def running_plane(z, carry):
        for x0, size in chunks(SPAN, 32):
            value = slope[z, pl.ds(x0, size), :]
            crow[z, pl.ds(x0, size), :] = running(value) - 0.5 * value
        return carry

    def slope_pack():
        def store(side, x0, size, value):
            spack[side, pl.ds(x0, size), :] = value

        pack_field(lambda z, x0, size: slope[z, pl.ds(x0, size), :], store, SPAN)
        for side, target in ((0, down_gy), (1, up_gy)):
            y_copies.append(pltpu.make_async_remote_copy(
                src_ref=spack.at[side], dst_ref=sland.at[side],
                send_sem=y_send.at[1, side], recv_sem=y_recv.at[1, side],
                device_id={"gy": target}, device_id_type=MESH))
            y_copies[-1].start()
        for x0, size in chunks(SPAN, 32):
            slot = lanes((size, L)) // 4

            def body(z, carry):
                line = jnp.sum(slope[z, pl.ds(x0, size), :], axis=1, keepdims=True)
                return jnp.where(slot == z, line, carry)

            tot_pack[pl.ds(x0, size), :] = lax.fori_loop(0, depth, body, jnp.zeros((size, L), F32))

    def work(stage):
        if stage == 0:
            slope_pack()
            lax.fori_loop(0, depth, running_plane, 0)
        cut = [0] + [depth * k // len(rings) for k in range(1, len(rings))] + [depth]
        lax.fori_loop(cut[stage], cut[stage + 1], plane_terms, 0)

    below = jnp.zeros((8 * GROUPS, L), F32)
    for stage, (stride, size) in enumerate(rings):
        stage_out[stage] = own
        copies = send_stage(stage)
        work(stage)
        mine = lax.rem(gy // stride, size)
        for copy in copies:
            copy.wait()
        own = stage_out[stage]
        for o in range(1, size):
            sender = lax.rem(mine + size - o, size)
            value = stage_in[stage, o - 1]
            own = own + value
            below = below + jnp.where(sender < mine, value, 0.0)
        if stage < len(rings) - 1:
            below_total[0] = below
            below = below_total[0]
    below_total[0] = below
    below_total[1] = own

    for copy in y_copies:
        copy.wait()
    for x0, size in chunks(SPAN, 32):
        within = lax.rem(lanes((size, L)), 4)
        own_rows = pl.ds(x0, size)
        total_line = tot_pack[own_rows, :]

        def from_start(values):
            result = 0.5 * values
            for k in range(1, 4):
                result = result + jnp.where(within >= k, rolled(values, k), 0.0)
            return result

        def to_end(values):
            result = 0.5 * values
            for k in range(1, 4):
                result = result + jnp.where(within <= 3 - k, rolled(values, -k), 0.0)
            return result

        chalo[FRONT, own_rows, :] = from_start(spack[0, own_rows, :])
        chalo[BACK, own_rows, :] = total_line - to_end(spack[1, own_rows, :])
        chalo[NEXT, own_rows, :] = total_line + from_start(sland[0, own_rows, :])
        chalo[PREV, own_rows, :] = -to_end(sland[1, own_rows, :])


def second_kernel(
    depth, uw, crow, halo, chalo, part, below_total, rows, m120,
    out, vel, result, vslots, edges, out_sem,
):
    frac = rows[ROW_FRAC][0:1]

    def around(z, d):
        return lax.rem(z + (depth + d), depth)

    lane_from = lax.broadcasted_iota(jnp.int32, (L, L), 0)
    plane_to = lanes((L, L)) // 4
    both = below_total[...].reshape(2 * 8 * GROUPS, L)
    for quarter in range(4):
        pick = (lane_from == 32 * quarter + plane_to).astype(F32)
        spread = jnp.dot(both, pick, precision=lax.Precision.HIGHEST, preferred_element_type=F32)
        for group in range(GROUPS):
            tile = 4 * group + quarter
            if tile >= TILES:
                continue
            rows_of = pl.ds(8 * tile, 8)
            below = spread[8 * group:8 * group + 8]
            total = spread[8 * (GROUPS + group):8 * (GROUPS + group) + 8]
            for n in range(4):
                vslots[n, rows_of, :] = rows[ROW_SLOTS + n] * total - (chalo[n, rows_of, :] + below)

    for x0, size in chunks(L, 32):
        own, own_v = pl.ds(x0, size), pl.ds(EDGE + x0, size)
        for side, here, there, first in ((0, FRONT, PREV, 3), (1, BACK, NEXT, 0)):
            centre = vslots[here, own_v, :]
            away = [halo[1 - side, 0, own, :], vslots[there, own_v, :], halo[1 - side, 1, own, :]]
            sums = [None] * 3
            for d in range(1, 4):
                near = [rolled(x, 4 - d if side else d - 4) for x in away]
                factor = rows[ROW_EDGES + first + d - 1][0:1] * (centre + near[1])
                for f in range(3):
                    term = factor * near[f]
                    sums[f] = term if sums[f] is None else sums[f] + term
            for f in range(3):
                edges[side, f, own, :] = sums[f]

    def column(which, z, x0, size):
        pieces = []
        for t in range(size // 8):
            tile = x0 // 8 + t
            group, quarter = tile // 4, tile % 4
            values = below_total[which, pl.ds(8 * group, 8), :]
            turned = pltpu.roll(values, lax.rem(2 * L - 32 * quarter - z, L), 1)
            pieces.append(jnp.broadcast_to(turned[:, 0:1], (8, L)))
        return jnp.concatenate(pieces, axis=0)

    def normal_plane(z, carry):
        for x0, size in chunks(SPAN, 32):
            own = pl.ds(x0, size)
            below, total = column(0, z, x0, size), column(1, z, x0, size)
            vel[z, own, :] = frac * total - (crow[z, own, :] + below)
        return carry

    lax.fori_loop(0, depth, normal_plane, 0)

    def plane(z, carry):
        to_front, to_back = lax.rem(L - 4 * z, L), lax.rem(2 * L - 4 - 4 * z, L)
        for x0, size in chunks(L, STEP):
            lane = lanes((size, L))
            own = pl.ds(x0, size)

            def at(d):
                return vel[z, pl.ds(EDGE + x0 + d, size), :]

            def over(d):
                return vel[around(z, d), pl.ds(EDGE + x0, size), :]

            def q_at(d):
                return uw[0, z, pl.ds(HALO + x0 + d, size), :]

            def q_over(d):
                return uw[1, around(z, d), pl.ds(HALO + x0, size), :]

            (along_x,) = skew(q_at, (at,))
            (along_z,) = skew(q_over, (over,))
            sums = [part[0, z, own, :], m120[own, :] * along_x + along_z * (1.0 / 120.0), part[1, z, own, :]]
            fields = [q_at(0), at(0), q_over(0)]
            for k in range(7):
                near = [rolled(x, 3 - k) for x in fields]
                factor = rows[k][0:1] * (fields[1] + near[1])
                for f in range(3):
                    sums[f] = sums[f] + factor * near[f]
            for f in range(3):
                edge = jnp.where(lane >= L - 4, pltpu.roll(edges[1, f, own, :], to_back, 1), 0.0)
                edge = jnp.where(lane < 4, pltpu.roll(edges[0, f, own, :], to_front, 1), edge)
                result[z, f, own, :] = sums[f] + edge
        pltpu.make_async_copy(result.at[z], out.at[:, z], out_sem.at[z]).start()
        return carry

    lax.fori_loop(0, depth, plane, 0)

    def finish(z, carry):
        pltpu.make_async_copy(result.at[z], out.at[:, z], out_sem.at[z]).wait()
        return carry

    lax.fori_loop(0, depth, finish, 0)


def shards(n_gy, velocity, stream_metric, wall_metric):
    depth = velocity.shape[1]
    n_ring = len(rings_of(n_gy))
    others = max(size for _, size in rings_of(n_gy)) - 1
    kept = [
        (2, depth, WIDE, L),
        (depth, SPAN, L),
        (2, 2, L, L),
        (4, SPAN, L),
        (2, depth, L, L),
        (2, 8 * GROUPS, L),
        (ROWS, 8, L),
        (L, L),
    ]
    here = pl.BlockSpec(memory_space=pltpu.VMEM)
    anywhere = pl.BlockSpec(memory_space=pl.ANY)
    dma = pltpu.SemaphoreType.DMA
    held = pl.pallas_call(
        functools.partial(first_kernel, n_gy, depth),
        out_shape=[KEEP(shape) for shape in kept],
        in_specs=[pl.BlockSpec(memory_space=pltpu.HBM), here, here],
        out_specs=[here] * len(kept),
        scratch_shapes=[
            pltpu.VMEM((depth, SPAN, L), F32),
            pltpu.VMEM((WIDE, L), F32),
            pltpu.VMEM((2, 2, L, L), F32),
            pltpu.VMEM((2, SPAN, L), F32),
            pltpu.VMEM((2, SPAN, L), F32),
            pltpu.VMEM((n_ring, 8 * GROUPS, L), F32),
            pltpu.VMEM((n_ring, others, 8 * GROUPS, L), F32),
            pltpu.VMEM((SPAN, L), F32),
            dma((2, 2)), dma((2, 2)), dma((2, 2)), dma((2, 2)), dma((2, 2)),
            dma((n_ring, others)), dma((n_ring, others)),
        ],
        compiler_params=pltpu.CompilerParams(
            collective_id=0, has_side_effects=True, vmem_limit_bytes=VMEM_FIRST),
        name="exchange",
    )(velocity, stream_metric.reshape(2, L), wall_metric.reshape(n_gy, L))
    return pl.pallas_call(
        functools.partial(second_kernel, depth),
        out_shape=jax.ShapeDtypeStruct((3, depth, L, L), F32),
        in_specs=[here] * len(kept),
        out_specs=anywhere,
        scratch_shapes=[
            pltpu.VMEM((depth, SPAN, L), F32),
            pltpu.VMEM((depth, 3, L, L), F32),
            pltpu.VMEM((4, SPAN, L), F32),
            pltpu.VMEM((2, 3, L, L), F32),
            dma((depth,)),
        ],
        compiler_params=pltpu.CompilerParams(vmem_limit_bytes=VMEM_SECOND),
        name="advect",
    )(*held)


STEP = 32
VMEM_FIRST = 16 * 2**20
VMEM_SECOND = 20 * 2**20


def KEEP(shape):
    return jax.ShapeDtypeStruct(shape, F32)


def solution(mesh):
    spec = P(None, None, "gx", "gy")
    return jax.shard_map(
        functools.partial(shards, mesh.shape["gy"]), mesh=mesh,
        in_specs=(spec, P(), P()), out_specs=spec, check_vma=False)
```

```python
import functools

import jax
import jax.numpy as jnp
from jax import lax
from jax.experimental import pallas as pl
from jax.experimental.pallas import tpu as pltpu
from jax.sharding import PartitionSpec as P

MESH = pl.DeviceIdType.MESH
F32, BF16 = jnp.float32, jnp.bfloat16
L = 128
HALO = 8
EDGE = 4
WIDE = L + 2 * HALO
SPAN = L + 2 * EDGE
CENTRAL = (45.0, -9.0, 1.0)
INTERIOR = (-1.0, 9.0, -45.0, 0.0, 45.0, -9.0, 1.0)
ROW_FIRST = (0.0, 0.0, 0.0, -110.0, 180.0, -90.0, 20.0)
ROW_SECOND = (0.0, 0.0, -20.0, -30.0, 60.0, -10.0, 0.0)
ROW_THIRD = (0.0, 5.0, -40.0, 0.0, 40.0, -5.0, 0.0)
ROW_SECOND_LAST = (0.0, 10.0, -60.0, 30.0, 20.0, 0.0, 0.0)
ROW_LAST = (-20.0, 90.0, -180.0, 110.0, 0.0, 0.0, 0.0)
TILES = SPAN // 8
GROUPS = -(-TILES // 4)
PACKED = 8 * GROUPS
SLOT, HALF = 8, 16
ROW_FRAC, ROW_SCALE, ROW_OWN, ROW_AWAY, ROW_AFTER, ROW_BEFORE, ROWS = 7, 8, 9, 10, 11, 14, 17


def rings_of(count):
    size = 4 if count % 4 == 0 and count > 16 else 2
    rings, stride = [], 1
    while stride < count:
        rings.append((stride, size))
        stride *= size
    return rings


def lanes(shape):
    return lax.broadcasted_iota(jnp.int32, shape, len(shape) - 1)


def rolled(x, shift):
    if isinstance(shift, int):
        shift %= L
        if shift == 0:
            return x
    return pltpu.roll(x, shift, len(x.shape) - 1)


def running(x):
    lane = lanes(x.shape)
    step = 1
    while step < L:
        x = x + jnp.where(lane >= step, rolled(x, step), 0.0)
        step *= 2
    return x


def scaled(x, weight):
    return x if weight == 1.0 else x * weight


def chunks(total, size):
    return [(min(i, total - size), size) for i in range(0, total, size)]


def pieces(x):
    high = x.astype(BF16)
    rest = x - high.astype(F32)
    middle = rest.astype(BF16)
    low = (rest - middle.astype(F32)).astype(BF16)
    return jnp.concatenate([high, middle, low], axis=1)


def skew(adv, fields):
    centre = adv(0)
    sums = [None] * len(fields)
    for d, weight in enumerate(CENTRAL, start=1):
        up = scaled(centre + adv(d), weight)
        down = scaled(centre + adv(-d), weight)
        for n, field in enumerate(fields):
            term = up * field(d) - down * field(-d)
            sums[n] = term if sums[n] is None else sums[n] + term
    return sums


def slope_sum(field):
    total = None
    for d, weight in enumerate(CENTRAL, start=1):
        term = scaled(field(d) - field(-d), weight)
        total = term if total is None else total + term
    return total


def first_kernel(
    n_gy, depth,
    vel, sm_far, wm_far,
    uw, crow, halo, shalo, part, lines, rows, m120,
    slope, m_wide, ladder, stage_out, stage_in, sm, wm, left_even, left_odd,
    load_sem, gx_send, gx_recv, y_send, y_recv, st_send, st_recv,
):
    gx, gy = lax.axis_index("gx"), lax.axis_index("gy")
    other = 1 - gx
    rings = rings_of(n_gy)
    up_gy, down_gy = lax.rem(gy + 1, n_gy), lax.rem(gy + n_gy - 1, n_gy)
    half = min(HALF, depth)
    halves = depth // half

    def peer(stride, size, offset):
        place = lax.rem(gy // stride, size)
        return gy + (lax.rem(place + offset, size) - place) * stride

    small = [pltpu.make_async_copy(sm_far, sm, load_sem.at[2]), pltpu.make_async_copy(wm_far, wm, load_sem.at[3])]
    for copy in small:
        copy.start()
    loads = []
    for f in range(2):
        loads.append(pltpu.make_async_copy(vel.at[f], uw.at[f, :, pl.ds(HALO, L)], load_sem.at[f]))
        loads[-1].start()

    barrier = pltpu.get_barrier_semaphore()
    count = 0
    targets = [{"gx": other}, {"gy": up_gy}, {"gy": down_gy}]
    for stride, size in rings:
        targets += [{"gy": peer(stride, size, o)} for o in range(1, size)]
    for target in targets:
        pl.semaphore_signal(barrier, inc=1, device_id=target, device_id_type=MESH)
        count += 1

    for copy in small:
        copy.wait()
    rid = lax.broadcasted_iota(jnp.int32, (n_gy, L), 0)
    wall = wm[...]
    recip = 1.0 / wall

    def row_at(values, index):
        picked = jnp.sum(jnp.where(rid == index, values, 0.0), axis=0, keepdims=True)
        return jnp.broadcast_to(picked, (8, L))

    def whole(values):
        return jnp.sum(jnp.sum(values, axis=0, keepdims=True), axis=1, keepdims=True)

    total_h = whole(recip)
    below_h = whole(jnp.where(rid < gy, recip, 0.0))
    r_own, r_next, r_prev = row_at(recip, gy), row_at(recip, up_gy), row_at(recip, down_gy)
    wall_own = row_at(wall, gy)
    lane8 = lanes((8, L))
    run_own, run_next, run_prev = running(r_own), running(r_next), running(r_prev)
    sum_own = jnp.sum(r_own[0:1], axis=1, keepdims=True)
    sum_prev = jnp.sum(r_prev[0:1], axis=1, keepdims=True)
    frac = (below_h + (run_own - 0.5 * r_own)) / total_h
    frac_next = (below_h + sum_own + (run_next - 0.5 * r_next)) / total_h
    frac_prev = (below_h - sum_prev + (run_prev - 0.5 * r_prev)) / total_h
    scale = wall_own * (1.0 / 120.0)
    rows[ROW_FRAC] = frac
    rows[ROW_SCALE] = scale
    within8 = lax.rem(lane8, SLOT)

    def slots(last, first):
        values = jnp.where(lane8 < 4, rolled(last, 4), 0.0)
        values = values + jnp.where((lane8 >= 4) & (lane8 < 8), rolled(first, 4), 0.0)
        step = SLOT
        while step < L:
            values = values + rolled(values, step)
            step *= 2
        return values

    rows[ROW_OWN] = slots(frac, frac)
    rows[ROW_AWAY] = slots(frac_prev, frac_next)
    place = gy * L + lane8
    last_row = n_gy * L - 1
    for k in range(7):
        entry = jnp.full((8, L), INTERIOR[k], F32)
        for row, table in ((0, ROW_FIRST), (1, ROW_SECOND), (2, ROW_THIRD), (last_row - 2, ROW_THIRD),
                           (last_row - 1, ROW_SECOND_LAST), (last_row, ROW_LAST)):
            entry = jnp.where(place == row, table[k], entry)
        rows[k] = entry
        d = k - 3
        if d != 0:
            both = slots(entry * scale, entry * scale)
        if d > 0:
            rows[ROW_AFTER + d - 1] = jnp.where((within8 < 4) & (within8 + d >= 4), both, 0.0)
        if d < 0:
            rows[ROW_BEFORE - d - 1] = jnp.where((within8 >= 4) & (within8 + d < 4), both, 0.0)
    r60 = r_own[0:1] * (1.0 / 60.0)

    first_row, second_row = sm[0:1, :], sm[1:2, :]
    own_m = jnp.where(gx == 0, first_row, second_row)
    other_m = jnp.where(gx == 0, second_row, first_row)
    own_cols = jnp.broadcast_to(own_m, (L, L)).T
    other_cols = jnp.broadcast_to(other_m, (L, L)).T
    m_wide[0:HALO, :] = other_cols[L - HALO:L, :]
    m_wide[HALO:HALO + L, :] = own_cols
    m_wide[HALO + L:WIDE, :] = other_cols[0:HALO, :]
    m120[...] = own_cols * (1.0 / 120.0)
    source = lax.broadcasted_iota(jnp.int32, (L, 2 * L), 0)
    target = lanes((L, 2 * L))
    steps = jnp.where(source < target, 1.0, jnp.where(source == target, 0.5, 0.0)).astype(BF16)
    for n in range(3):
        ladder[n * L:(n + 1) * L, :] = steps

    pl.semaphore_wait(barrier, count)

    gx_copies = []
    for f in range(2):
        for side, (src, dst) in enumerate(((L - HALO, 0), (0, HALO + L))):
            gx_copies.append(pltpu.make_async_remote_copy(
                src_ref=vel.at[f, :, pl.ds(src, HALO)], dst_ref=uw.at[f, :, pl.ds(dst, HALO)],
                send_sem=gx_send.at[f, side], recv_sem=gx_recv.at[f, side],
                device_id={"gx": other}, device_id_type=MESH))
            gx_copies[-1].start()

    for copy in loads:
        copy.wait()

    def send_slots(array, n):
        copies = []
        for side, where in ((1, down_gy), (2, up_gy)):
            copies.append(pltpu.make_async_remote_copy(
                src_ref=array.at[0], dst_ref=array.at[side],
                send_sem=y_send.at[n, side - 1], recv_sem=y_recv.at[n, side - 1],
                device_id={"gy": where}, device_id_type=MESH))
            copies[-1].start()
        return copies

    def pack(read, extent, store):
        slot = lanes((extent, L)) // SLOT
        for h in range(halves):
            def body(z, packed):
                return jnp.where(slot == z, pltpu.roll(read(h * half + z), SLOT * z + 4, 1), packed)

            store(h, lax.fori_loop(0, half, body, jnp.zeros((extent, L), F32), unroll=4))

    for f in range(2):
        def store_halo(h, value, f=f):
            halo[0, f, h] = value

        pack(lambda z, f=f: uw[f, z, pl.ds(HALO, L), :], L, store_halo)
    y_copies = send_slots(halo, 0)

    for copy in gx_copies:
        copy.wait()

    lane_small = lanes((8, L))
    shift = HALO - EDGE

    def around(z, d):
        return lax.rem(z + (depth + d), depth)

    def slope_split(z, left):
        for x0, size in chunks(SPAN, 48):
            du = slope_sum(lambda d: uw[0, z, pl.ds(shift + x0 + d, size), :])
            dw = slope_sum(lambda d: uw[1, around(z, d), pl.ds(shift + x0, size), :])
            value = (m_wide[pl.ds(shift + x0, size), :] * du + dw) * r60
            slope[z, pl.ds(x0, size), :] = value
            left[pl.ds(min(x0, SPAN - size) + (SLOT if x0 + size == SPAN else 0), size), :] = pieces(value)

    def row_in_left(row):
        return row if row < SPAN - 48 else row + SLOT

    def slope_climb(z, left, sums):
        climbed = jnp.dot(left[...], ladder[...], preferred_element_type=F32)
        for tile in range(TILES):
            row = row_in_left(8 * tile)
            crow[z, pl.ds(8 * tile, 8), :] = climbed[row:row + 8, :L]
            group, quarter = tile // 4, tile % 4
            sums[group] = jnp.where(lane_small == 32 * quarter + z, climbed[row:row + 8, L:], sums[group])
        return sums

    slope_split(0, left_even)

    def slope_plane(n, sums):
        z = 2 * n
        slope_split(z + 1, left_odd)
        sums = slope_climb(z, left_even, list(sums))
        slope_split(around(z, 2), left_even)
        return tuple(slope_climb(z + 1, left_odd, sums))

    sums = lax.fori_loop(0, depth // 2, slope_plane, tuple(jnp.zeros((8, L), F32) for _ in range(GROUPS)))
    own = jnp.concatenate(sums, axis=0)
    lines[2] = own

    def send_stage(stage):
        stride, size = rings[stage]
        copies = []
        for o in range(1, size):
            copies.append(pltpu.make_async_remote_copy(
                src_ref=stage_out.at[stage], dst_ref=stage_in.at[stage, o - 1],
                send_sem=st_send.at[stage, o - 1], recv_sem=st_recv.at[stage, o - 1],
                device_id={"gy": peer(stride, size, o)}, device_id_type=MESH))
            copies[-1].start()
        return copies

    def plane_terms(z, carry):
        for x0, size in chunks(L, 32):
            def at(f):
                return lambda d: uw[f, z, pl.ds(HALO + x0 + d, size), :]

            def over(f):
                return lambda d: uw[f, around(z, d), pl.ds(HALO + x0, size), :]

            along_x = skew(at(0), (at(0), at(1)))
            along_z = skew(over(1), (over(0), over(1)))
            m = m120[pl.ds(x0, size), :]
            for f in range(2):
                part[f, z, pl.ds(x0, size), :] = m * along_x[f] + along_z[f] * (1.0 / 120.0)
        return carry

    below = jnp.zeros((PACKED, L), F32)
    cut = [depth * k // len(rings) for k in range(len(rings) + 1)]
    for stage, (stride, size) in enumerate(rings):
        stage_out[stage] = own
        copies = send_stage(stage)
        if stage == 0:
            def store_slope(h, value):
                shalo[0, h] = value

            pack(lambda z: slope[z], SPAN, store_slope)
            y_copies += send_slots(shalo, 1)
        lax.fori_loop(cut[stage], cut[stage + 1], plane_terms, 0)
        mine = lax.rem(gy // stride, size)
        for copy in copies:
            copy.wait()
        own = stage_out[stage]
        for o in range(1, size):
            sender = lax.rem(mine + size - o, size)
            value = stage_in[stage, o - 1]
            own = own + value
            below = below + jnp.where(sender < mine, value, 0.0)
        if stage < len(rings) - 1:
            lines[0] = below
            below = lines[0]
    lines[0] = below
    lines[1] = own

    for copy in y_copies:
        copy.wait()


def second_kernel(
    depth, uw, crow, halo, shalo, part, lines, rows, m120,
    out, vel, result, spread, vslots, edges, picks, weights,
    left_even, left_odd, right_even, right_odd, out_sem,
):
    half = min(HALF, depth)
    halves = depth // half
    frac = rows[ROW_FRAC][0:1]
    scale = rows[ROW_SCALE][0:1]

    def around(z, d):
        return lax.rem(z + (depth + d), depth)

    source = lax.broadcasted_iota(jnp.int32, (L, L), 0)
    target = lanes((L, L))
    stencil = jnp.zeros((L, L), F32)
    for k in range(7):
        stencil = jnp.where(source - target == k - 3, rows[k][0:1], stencil)
    stencil = stencil.astype(BF16)
    for n in range(3):
        weights[n * L:(n + 1) * L, :] = stencil

    packed = pieces(lines[...].reshape(3 * PACKED, L))
    for quarter in range(4):
        for h in range(halves):
            pick = (source == 32 * quarter + half * h + target // SLOT).astype(F32).astype(BF16)
            for n in range(3):
                picks[n * L:(n + 1) * L, :] = pick
            found = jnp.dot(packed, picks[...], preferred_element_type=F32)
            for group in range(GROUPS):
                tile = 4 * group + quarter
                if tile < TILES:
                    for n in range(3):
                        at = n * PACKED + 8 * group
                        spread[n, h, pl.ds(8 * tile, 8), :] = found[at:at + 8]

    for h in range(halves):
        for x0, size in chunks(SPAN, 8 * 17):
            area = pl.ds(x0, size)
            within = lax.rem(lanes((size, L)), SLOT)
            first_rows = within >= 4
            below, total, line = (spread[n, h, area, :] for n in range(3))

            def local(values):
                result = 0.5 * values
                for k in range(1, 4):
                    result = result + jnp.where(within >= 4 + k, rolled(values, k), 0.0)
                    result = result + jnp.where(within <= 3 - k, rolled(values, -k), 0.0)
                return result

            near = local(shalo[0, h, area, :])
            away = local(jnp.where(first_rows, shalo[1, h, area, :], shalo[2, h, area, :]))
            near = jnp.where(first_rows, near, line - near)
            away = jnp.where(first_rows, line + away, -away)
            vslots[0, h, area, :] = rows[ROW_OWN][0:1] * total - (near + below)
            vslots[1, h, area, :] = rows[ROW_AWAY][0:1] * total - (away + below)

    for h in range(halves):
        for x0, size in chunks(L, 32):
            area, area_v = pl.ds(x0, size), pl.ds(EDGE + x0, size)
            first_rows = lax.rem(lanes((size, L)), SLOT) >= 4
            centre = vslots[0, h, area_v, :]
            away = [jnp.where(first_rows, halo[1, f, h, area, :], halo[2, f, h, area, :]) for f in range(2)]
            away = [away[0], vslots[1, h, area_v, :], away[1]]
            sums = [None] * 3
            for d in range(1, 4):
                for row, turn in ((ROW_AFTER, -d), (ROW_BEFORE, d)):
                    near = [rolled(x, turn) for x in away]
                    factor = rows[row + d - 1][0:1] * (centre + near[1])
                    for f in range(3):
                        term = factor * near[f]
                        sums[f] = term if sums[f] is None else sums[f] + term
            for f in range(3):
                edges[h, f, area, :] = sums[f]

    def normal_plane(z, carry):
        turn = lax.rem(L - z, L)
        turned = [[pltpu.roll(lines[n, pl.ds(8 * g, 8), :], turn, 1) for g in range(GROUPS)] for n in range(2)]
        for tile in range(TILES):
            group, at = tile // 4, 32 * (tile % 4)
            below, total = (jnp.broadcast_to(turned[n][group][:, at:at + 1], (8, L)) for n in range(2))
            area = pl.ds(8 * tile, 8)
            vel[z, area, :] = frac * total - (crow[z, area, :] + below)
        return carry

    lax.fori_loop(0, depth, normal_plane, 0, unroll=2)

    def at(z, x0, d):
        return vel[z, pl.ds(EDGE + x0 + d, STEP), :]

    def q_at(f, z, x0, d):
        return uw[f, z, pl.ds(HALO + x0 + d, STEP), :]

    def split(z, left):
        for x0 in range(0, L, STEP):
            v = at(z, x0, 0)
            for f, field in enumerate((q_at(0, z, x0, 0), v, q_at(1, z, x0, 0))):
                left[pl.ds(f * L + x0, STEP), :] = pieces(field)
                left[pl.ds((3 + f) * L + x0, STEP), :] = pieces(v * field)

    def plane(z, left, right, later):
        turn = lax.rem(2 * L - 4 - SLOT * lax.rem(z, half), L)
        right[...] = jnp.dot(left[...], weights[...], preferred_element_type=F32)
        if later is not None:
            split(*later)
        for x0 in range(0, L, STEP):
            own = pl.ds(x0, STEP)
            (along_x,) = skew(lambda d: q_at(0, z, x0, d), (lambda d: at(z, x0, d),))
            (along_z,) = skew(lambda d: q_at(1, around(z, d), x0, 0), (lambda d: at(around(z, d), x0, 0),))
            result[z, 1, own, :] = m120[own, :] * along_x + along_z * (1.0 / 120.0)
        for x0 in range(0, L, STEP):
            own = pl.ds(x0, STEP)
            lane = lanes((STEP, L))
            v = at(z, x0, 0)
            for f in range(3):
                others = result[z, 1, own, :] if f == 1 else part[f // 2, z, own, :]
                turned = pltpu.roll(edges[z // half, f, own, :], turn, 1)
                edge = jnp.where((lane < 4) | (lane >= L - 4), turned, 0.0)
                slope, flux = right[pl.ds(f * L + x0, STEP), :], right[pl.ds((3 + f) * L + x0, STEP), :]
                result[z, f, own, :] = others + (v * slope + flux) * scale + edge
        pltpu.make_async_copy(result.at[z], out.at[:, z], out_sem.at[z]).start()

    split(0, left_even)

    def two_planes(n, carry):
        z = 2 * n
        plane(z, left_even, right_even, (z + 1, left_odd))
        plane(z + 1, left_odd, right_odd, (around(z, 2), left_even))
        return carry

    lax.fori_loop(0, depth // 2, two_planes, 0)

    def finish(z, carry):
        pltpu.make_async_copy(result.at[z], out.at[:, z], out_sem.at[z]).wait()
        return carry

    lax.fori_loop(0, depth, finish, 0)


STEP = 32
VMEM_FIRST = 24 * 2**20
VMEM_SECOND = 24 * 2**20


def shards(n_gy, velocity, stream_metric, wall_metric):
    depth = velocity.shape[1]
    halves = depth // min(HALF, depth)
    n_ring = len(rings_of(n_gy))
    others = max(size for _, size in rings_of(n_gy)) - 1
    kept = [
        (2, depth, WIDE, L),
        (depth, SPAN, L),
        (3, 2, halves, L, L),
        (3, halves, SPAN, L),
        (2, depth, L, L),
        (3, PACKED, L),
        (ROWS, 8, L),
        (L, L),
    ]
    here = pl.BlockSpec(memory_space=pltpu.VMEM)
    anywhere = pl.BlockSpec(memory_space=pl.ANY)
    dma = pltpu.SemaphoreType.DMA
    held = pl.pallas_call(
        functools.partial(first_kernel, n_gy, depth),
        out_shape=[pltpu.VMEM(shape, F32) for shape in kept],
        in_specs=[pl.BlockSpec(memory_space=pltpu.HBM)] * 3,
        out_specs=[here] * len(kept),
        scratch_shapes=[
            pltpu.VMEM((depth, SPAN, L), F32),
            pltpu.VMEM((WIDE, L), F32),
            pltpu.VMEM((3 * L, 2 * L), BF16),
            pltpu.VMEM((n_ring, PACKED, L), F32),
            pltpu.VMEM((n_ring, others, PACKED, L), F32),
            pltpu.VMEM((2, L), F32),
            pltpu.VMEM((n_gy, L), F32),
            pltpu.VMEM((WIDE, 3 * L), BF16),
            pltpu.VMEM((WIDE, 3 * L), BF16),
            dma((4,)), dma((2, 2)), dma((2, 2)), dma((2, 2)), dma((2, 2)),
            dma((n_ring, others)), dma((n_ring, others)),
        ],
        compiler_params=pltpu.CompilerParams(
            collective_id=0, has_side_effects=True, vmem_limit_bytes=VMEM_FIRST),
        name="exchange",
    )(*(pltpu.with_memory_space_constraint(x, pltpu.HBM)
        for x in (velocity, stream_metric.reshape(2, L), wall_metric.reshape(n_gy, L))))
    return pl.pallas_call(
        functools.partial(second_kernel, depth),
        out_shape=jax.ShapeDtypeStruct((3, depth, L, L), F32),
        in_specs=[here] * len(kept),
        out_specs=anywhere,
        scratch_shapes=[
            pltpu.VMEM((depth, SPAN, L), F32),
            pltpu.VMEM((depth, 3, L, L), F32),
            pltpu.VMEM((3, halves, SPAN, L), F32),
            pltpu.VMEM((2, halves, SPAN, L), F32),
            pltpu.VMEM((halves, 3, L, L), F32),
            pltpu.VMEM((3 * L, L), BF16),
            pltpu.VMEM((3 * L, L), BF16),
            pltpu.VMEM((6 * L, 3 * L), BF16),
            pltpu.VMEM((6 * L, 3 * L), BF16),
            pltpu.VMEM((6 * L, L), F32),
            pltpu.VMEM((6 * L, L), F32),
            dma((depth,)),
        ],
        compiler_params=pltpu.CompilerParams(vmem_limit_bytes=VMEM_SECOND),
        name="advect",
    )(*held)


def solution(mesh):
    spec = P(None, None, "gx", "gy")
    return jax.shard_map(
        functools.partial(shards, mesh.shape["gy"]), mesh=mesh,
        in_specs=(spec, P(), P()), out_specs=spec, check_vma=False)
```

```python
import functools

import jax
import jax.numpy as jnp
from jax import lax
from jax.experimental import pallas as pl
from jax.experimental.pallas import tpu as pltpu
from jax.sharding import PartitionSpec as P

MESH = pl.DeviceIdType.MESH
F32, BF16 = jnp.float32, jnp.bfloat16
L = 128
HALO = 8
EDGE = 4
WIDE = L + 2 * HALO
SPAN = L + 2 * EDGE
CENTRAL = (45.0, -9.0, 1.0)
INTERIOR = (-1.0, 9.0, -45.0, 0.0, 45.0, -9.0, 1.0)
ROW_FIRST = (0.0, 0.0, 0.0, -110.0, 180.0, -90.0, 20.0)
ROW_SECOND = (0.0, 0.0, -20.0, -30.0, 60.0, -10.0, 0.0)
ROW_THIRD = (0.0, 5.0, -40.0, 0.0, 40.0, -5.0, 0.0)
ROW_SECOND_LAST = (0.0, 10.0, -60.0, 30.0, 20.0, 0.0, 0.0)
ROW_LAST = (-20.0, 90.0, -180.0, 110.0, 0.0, 0.0, 0.0)
TILES = SPAN // 8
GROUPS = -(-TILES // 4)
PACKED = 8 * GROUPS
SLOT, HALF = 8, 16
ROW_FRAC, ROW_SCALE, ROW_OWN, ROW_AWAY, ROW_SLOT, ROW_SLOT_SCALE, ROWS = 7, 8, 9, 10, 11, 18, 19


def rings_of(count):
    size = 4 if count % 4 == 0 and count > 16 else 2
    rings, stride = [], 1
    while stride < count:
        rings.append((stride, size))
        stride *= size
    return rings


def lanes(shape):
    return lax.broadcasted_iota(jnp.int32, shape, len(shape) - 1)


def rolled(x, shift):
    if isinstance(shift, int):
        shift %= L
        if shift == 0:
            return x
    return pltpu.roll(x, shift, len(x.shape) - 1)


def running(x):
    lane = lanes(x.shape)
    step = 1
    while step < L:
        x = x + jnp.where(lane >= step, rolled(x, step), 0.0)
        step *= 2
    return x


def scaled(x, weight):
    return x if weight == 1.0 else x * weight


def chunks(total, size):
    return [(min(i, total - size), size) for i in range(0, total, size)]


def three(x):
    high = x.astype(BF16)
    rest = x - high.astype(F32)
    middle = rest.astype(BF16)
    low = (rest - middle.astype(F32)).astype(BF16)
    return high, middle, low


def pieces(x):
    return jnp.concatenate(three(x), axis=1)


def pieces_of_two(x, y):
    return jnp.concatenate([part for pair in zip(three(x), three(y)) for part in pair], axis=1)


def skew(adv, fields):
    centre = adv(0)
    sums = [None] * len(fields)
    if len(fields) == 1:
        total = None
        for d, weight in enumerate(CENTRAL, start=1):
            term = (centre + adv(d)) * fields[0](d) - (centre + adv(-d)) * fields[0](-d)
            total = scaled(term, weight) if total is None else total + scaled(term, weight)
        return [total]
    for d, weight in enumerate(CENTRAL, start=1):
        up = scaled(centre + adv(d), weight)
        down = scaled(centre + adv(-d), weight)
        for n, field in enumerate(fields):
            term = up * field(d) - down * field(-d)
            sums[n] = term if sums[n] is None else sums[n] + term
    return sums


def slope_sum(field):
    total = None
    for d, weight in enumerate(CENTRAL, start=1):
        term = scaled(field(d) - field(-d), weight)
        total = term if total is None else total + term
    return total


def first_kernel(
    n_gy, depth,
    vel, sm_far, wm_far,
    uw, crow, halo, shalo, part, lines, rows, m120,
    slope, m_wide, ladder, stage_out, stage_in, sm, wm, left_even, left_odd,
    load_sem, gx_send, gx_recv, y_send, y_recv, st_send, st_recv,
):
    gx, gy = lax.axis_index("gx"), lax.axis_index("gy")
    other = 1 - gx
    rings = rings_of(n_gy)
    up_gy, down_gy = lax.rem(gy + 1, n_gy), lax.rem(gy + n_gy - 1, n_gy)
    half = min(HALF, depth)
    halves = depth // half

    def peer(stride, size, offset):
        place = lax.rem(gy // stride, size)
        return gy + (lax.rem(place + offset, size) - place) * stride

    small = [pltpu.make_async_copy(sm_far, sm, load_sem.at[2]), pltpu.make_async_copy(wm_far, wm, load_sem.at[3])]
    for copy in small:
        copy.start()
    loads = []
    for f in range(2):
        loads.append(pltpu.make_async_copy(vel.at[f], uw.at[f, :, pl.ds(HALO, L)], load_sem.at[f]))
        loads[-1].start()

    barrier = pltpu.get_barrier_semaphore()
    count = 0
    targets = [{"gx": other}, {"gy": up_gy}, {"gy": down_gy}]
    for stride, size in rings:
        targets += [{"gy": peer(stride, size, o)} for o in range(1, size)]
    for target in targets:
        pl.semaphore_signal(barrier, inc=1, device_id=target, device_id_type=MESH)
        count += 1

    for copy in small:
        copy.wait()
    rid = lax.broadcasted_iota(jnp.int32, (n_gy, L), 0)
    wall = wm[...]
    recip = 1.0 / wall

    def row_at(values, index):
        picked = jnp.sum(jnp.where(rid == index, values, 0.0), axis=0, keepdims=True)
        return jnp.broadcast_to(picked, (8, L))

    def whole(values):
        return jnp.sum(jnp.sum(values, axis=0, keepdims=True), axis=1, keepdims=True)

    total_h = whole(recip)
    below_h = whole(jnp.where(rid < gy, recip, 0.0))
    r_own, r_next, r_prev = row_at(recip, gy), row_at(recip, up_gy), row_at(recip, down_gy)
    wall_own = row_at(wall, gy)
    lane8 = lanes((8, L))
    run_own, run_next, run_prev = running(r_own), running(r_next), running(r_prev)
    sum_own = jnp.sum(r_own[0:1], axis=1, keepdims=True)
    sum_prev = jnp.sum(r_prev[0:1], axis=1, keepdims=True)
    frac = (below_h + (run_own - 0.5 * r_own)) / total_h
    frac_next = (below_h + sum_own + (run_next - 0.5 * r_next)) / total_h
    frac_prev = (below_h - sum_prev + (run_prev - 0.5 * r_prev)) / total_h
    scale = wall_own * (1.0 / 120.0)
    rows[ROW_FRAC] = frac
    rows[ROW_SCALE] = scale

    def slots(last, first):
        values = jnp.where(lane8 < 4, rolled(last, 4), 0.0)
        values = values + jnp.where((lane8 >= 4) & (lane8 < 8), rolled(first, 4), 0.0)
        step = SLOT
        while step < L:
            values = values + rolled(values, step)
            step *= 2
        return values

    rows[ROW_OWN] = slots(frac, frac)
    rows[ROW_AWAY] = slots(frac_prev, frac_next)
    place = gy * L + lane8
    last_row = n_gy * L - 1
    for k in range(7):
        entry = jnp.full((8, L), INTERIOR[k], F32)
        for row, table in ((0, ROW_FIRST), (1, ROW_SECOND), (2, ROW_THIRD), (last_row - 2, ROW_THIRD),
                           (last_row - 1, ROW_SECOND_LAST), (last_row, ROW_LAST)):
            entry = jnp.where(place == row, table[k], entry)
        rows[k] = entry
        rows[ROW_SLOT + k] = slots(entry, entry)
    rows[ROW_SLOT_SCALE] = slots(scale, scale)
    r60 = r_own[0:1] * (1.0 / 60.0)

    first_row, second_row = sm[0:1, :], sm[1:2, :]
    own_m = jnp.where(gx == 0, first_row, second_row)
    other_m = jnp.where(gx == 0, second_row, first_row)
    own_cols = jnp.broadcast_to(own_m, (L, L)).T
    other_cols = jnp.broadcast_to(other_m, (L, L)).T
    m_wide[0:HALO, :] = other_cols[L - HALO:L, :]
    m_wide[HALO:HALO + L, :] = own_cols
    m_wide[HALO + L:WIDE, :] = other_cols[0:HALO, :]
    m120[...] = own_cols * (1.0 / 120.0)
    source = lax.broadcasted_iota(jnp.int32, (L, 2 * L), 0)
    target = lanes((L, 2 * L))
    steps = jnp.where(source < target, 1.0, jnp.where(source == target, 0.5, 0.0)).astype(BF16)
    for n in range(3):
        ladder[n * L:(n + 1) * L, :] = steps

    pl.semaphore_wait(barrier, count)

    gx_copies = []
    for f in range(2):
        for side, (src, dst) in enumerate(((L - HALO, 0), (0, HALO + L))):
            gx_copies.append(pltpu.make_async_remote_copy(
                src_ref=vel.at[f, :, pl.ds(src, HALO)], dst_ref=uw.at[f, :, pl.ds(dst, HALO)],
                send_sem=gx_send.at[f, side], recv_sem=gx_recv.at[f, side],
                device_id={"gx": other}, device_id_type=MESH))
            gx_copies[-1].start()

    for copy in loads:
        copy.wait()

    def send_slots(array, n):
        copies = []
        for side, where in ((1, down_gy), (2, up_gy)):
            copies.append(pltpu.make_async_remote_copy(
                src_ref=array.at[0], dst_ref=array.at[side],
                send_sem=y_send.at[n, side - 1], recv_sem=y_recv.at[n, side - 1],
                device_id={"gy": where}, device_id_type=MESH))
            copies[-1].start()
        return copies

    def pack(read, extent, store):
        slot = lanes((extent, L)) // SLOT
        for h in range(halves):
            def body(z, packed):
                return jnp.where(slot == z, pltpu.roll(read(h * half + z), SLOT * z + 4, 1), packed)

            store(h, lax.fori_loop(0, half, body, jnp.zeros((extent, L), F32), unroll=4))

    for copy in gx_copies:
        copy.wait()

    lane_small = lanes((8, L))
    shift = HALO - EDGE

    def around(z, d):
        return lax.rem(z + (depth + d), depth)

    def slope_split(z, left):
        for x0, size in chunks(SPAN, 48):
            du = slope_sum(lambda d: uw[0, z, pl.ds(shift + x0 + d, size), :])
            dw = slope_sum(lambda d: uw[1, around(z, d), pl.ds(shift + x0, size), :])
            value = (m_wide[pl.ds(shift + x0, size), :] * du + dw) * r60
            slope[z, pl.ds(x0, size), :] = value
            left[pl.ds(min(x0, SPAN - size) + (SLOT if x0 + size == SPAN else 0), size), :] = pieces(value)

    def row_in_left(row):
        return row if row < SPAN - 48 else row + SLOT

    def slope_climb(z, left, sums, later):
        climbed = jnp.dot(left[...], ladder[...], preferred_element_type=F32)
        slope_split(*later)
        for tile in range(TILES):
            row = row_in_left(8 * tile)
            crow[z, pl.ds(8 * tile, 8), :] = climbed[row:row + 8, :L]
            group, quarter = tile // 4, tile % 4
            sums[group] = jnp.where(lane_small == 32 * quarter + z, climbed[row:row + 8, L:], sums[group])
        return sums

    slope_split(0, left_even)

    def slope_plane(n, sums):
        z = 2 * n
        sums = slope_climb(z, left_even, list(sums), (z + 1, left_odd))
        return tuple(slope_climb(z + 1, left_odd, sums, (around(z, 2), left_even)))

    sums = lax.fori_loop(0, depth // 2, slope_plane, tuple(jnp.zeros((8, L), F32) for _ in range(GROUPS)))
    own = jnp.concatenate(sums, axis=0)
    lines[2] = own

    def send_stage(stage):
        stride, size = rings[stage]
        copies = []
        for o in range(1, size):
            copies.append(pltpu.make_async_remote_copy(
                src_ref=stage_out.at[stage], dst_ref=stage_in.at[stage, o - 1],
                send_sem=st_send.at[stage, o - 1], recv_sem=st_recv.at[stage, o - 1],
                device_id={"gy": peer(stride, size, o)}, device_id_type=MESH))
            copies[-1].start()
        return copies

    def plane_terms(z, carry):
        for x0, size in chunks(L, 16):
            def at(f):
                return lambda d: uw[f, z, pl.ds(HALO + x0 + d, size), :]

            def over(f):
                return lambda d: uw[f, around(z, d), pl.ds(HALO + x0, size), :]

            along_x = skew(at(0), (at(0), at(1)))
            along_z = skew(over(1), (over(0), over(1)))
            m = m120[pl.ds(x0, size), :]
            for f in range(2):
                part[f, z, pl.ds(x0, size), :] = m * along_x[f] + along_z[f] * (1.0 / 120.0)
        return carry

    below = jnp.zeros((PACKED, L), F32)
    cut = [depth * k // len(rings) for k in range(len(rings) + 1)]
    for stage, (stride, size) in enumerate(rings):
        stage_out[stage] = own
        copies = send_stage(stage)
        if stage == 0:
            def store_slope(h, value):
                shalo[0, h] = value

            for f in range(2):
                def store_halo(h, value, f=f):
                    halo[0, f, h] = value

                pack(lambda z, f=f: uw[f, z, pl.ds(HALO, L), :], L, store_halo)
            y_copies = send_slots(halo, 0)
            pack(lambda z: slope[z], SPAN, store_slope)
            y_copies += send_slots(shalo, 1)
        lax.fori_loop(cut[stage], cut[stage + 1], plane_terms, 0)
        mine = lax.rem(gy // stride, size)
        for copy in copies:
            copy.wait()
        own = stage_out[stage]
        for o in range(1, size):
            sender = lax.rem(mine + size - o, size)
            value = stage_in[stage, o - 1]
            own = own + value
            below = below + jnp.where(sender < mine, value, 0.0)
        if stage < len(rings) - 1:
            lines[0] = below
            below = lines[0]
    lines[0] = below
    lines[1] = own

    for copy in y_copies:
        copy.wait()


def second_kernel(
    depth, uw, crow, halo, shalo, part, lines, rows, m120,
    out, vel, result, parts, vslots, edges, weights,
    left_even, left_odd, right_even, right_odd, out_sem,
):
    half = min(HALF, depth)
    halves = depth // half
    frac = rows[ROW_FRAC][0:1]
    scale = rows[ROW_SCALE][0:1]

    def around(z, d):
        return lax.rem(z + (depth + d), depth)

    source = lax.broadcasted_iota(jnp.int32, (L, L), 0)
    target = lanes((L, L))

    def store_weights(ref, matrix):
        matrix = matrix.astype(BF16)
        nothing = jnp.zeros((L, L), BF16)
        for n in range(3):
            ref[2 * n * L:(2 * n + 1) * L, :] = jnp.concatenate([matrix, nothing], axis=1)
            ref[(2 * n + 1) * L:(2 * n + 2) * L, :] = jnp.concatenate([nothing, matrix], axis=1)

    packed = pieces(lines[...].reshape(3 * PACKED, L))
    from_lane = lax.broadcasted_iota(jnp.int32, (3 * L, L), 0)
    to_lane = lanes((3 * L, L))
    for quarter in range(4):
        pick = (from_lane // L == to_lane // 32) & (lax.rem(from_lane, L) == 32 * quarter + lax.rem(to_lane, 32))
        found = jnp.dot(packed, pick.astype(F32).astype(BF16), preferred_element_type=F32)
        for group in range(GROUPS):
            tile = 4 * group + quarter
            if tile < TILES:
                for n in range(3):
                    at = n * PACKED + 8 * group
                    parts[n, pl.ds(8 * tile, 8), :] = found[at:at + 8]
    for n in range(3):
        parts[n, pl.ds(SPAN, 8), :] = jnp.zeros((8, L), F32)
    source2 = lax.broadcasted_iota(jnp.int32, (L, halves * L), 0)
    target2 = lanes((L, halves * L))
    to_slot = (lax.rem(source2, 32) == half * (target2 // L) + lax.rem(target2, L) // SLOT) & (source2 < 96)
    to_slot = to_slot.astype(F32).astype(BF16)

    same_slot = source // SLOT == target // SLOT
    place, aim = lax.rem(source, SLOT), lax.rem(target, SLOT)
    passed = ((place >= 4) & (place < aim)) | ((place < 4) & (place > aim))
    same_side = same_slot & ((place >= 4) == (aim >= 4))
    local = jnp.where(same_side & passed, 1.0, jnp.where(source == target, 0.5, 0.0)).astype(BF16)
    local = jnp.concatenate([local, local, local], axis=0)
    first_rows = lax.rem(lanes((SPAN, L)), SLOT) >= 4
    spread = [jnp.dot(parts[n].astype(BF16), to_slot, preferred_element_type=F32) for n in range(3)]
    for h in range(halves):
        below, total, line = (x[:SPAN, h * L:(h + 1) * L] for x in spread)
        near = jnp.dot(pieces(shalo[0, h]), local, preferred_element_type=F32)
        away = jnp.where(first_rows, shalo[1, h], shalo[2, h])
        away = jnp.dot(pieces(away), local, preferred_element_type=F32)
        near = jnp.where(first_rows, near, line - near)
        away = jnp.where(first_rows, line + away, -away)
        vslots[0, h] = rows[ROW_OWN][0:1] * total - (near + below)
        vslots[1, h] = rows[ROW_AWAY][0:1] * total - (away + below)

    across = same_slot & ((place >= 4) != (aim >= 4))
    stencil = jnp.zeros((L, L), F32)
    for k in range(7):
        stencil = jnp.where(across & (source - target == k - 3), rows[ROW_SLOT + k][0:1], stencil)
    store_weights(weights, stencil)
    scale8 = rows[ROW_SLOT_SCALE][0:1]
    for h in range(halves):
        for x0, size in chunks(L, 32):
            area = pl.ds(x0, size)
            first = lax.rem(lanes((size, L)), SLOT) >= 4
            v = vslots[1, h, pl.ds(EDGE + x0, size), :]
            away = [jnp.where(first, halo[1, f, h, area, :], halo[2, f, h, area, :]) for f in range(2)]
            for f, field in enumerate((away[0], v, away[1])):
                left_even[pl.ds(f * L + x0, size), :] = pieces_of_two(field, v * field)
        right_even[...] = jnp.dot(left_even[...], weights[...], preferred_element_type=F32)
        for x0, size in chunks(L, 32):
            v = vslots[0, h, pl.ds(EDGE + x0, size), :]
            for f in range(3):
                both = right_even[pl.ds(f * L + x0, size), :]
                edges[h, f, pl.ds(x0, size), :] = (v * both[:, :L] + both[:, L:]) * scale8

    stencil = jnp.zeros((L, L), F32)
    for k in range(7):
        stencil = jnp.where(source - target == k - 3, rows[k][0:1], stencil)
    store_weights(weights, stencil)

    source3 = lax.broadcasted_iota(jnp.int32, (2 * L, 2 * L), 0)
    target3 = lanes((2 * L, 2 * L))
    ones = (source3 // L == target3 // L).astype(F32).astype(BF16)
    both = jnp.concatenate([parts[0], parts[1]], axis=1)
    plane_of = lax.rem(lanes((WIDE, 2 * L)), 32)
    group_planes = 4

    def normal_planes(n, carry):
        z0 = group_planes * n
        chosen = [jnp.where(plane_of == z0 + k, both, 0.0).astype(BF16) for k in range(group_planes)]
        found = jnp.dot(jnp.concatenate(chosen, axis=0), ones, preferred_element_type=F32)
        for k in range(group_planes):
            here = found[k * WIDE:k * WIDE + SPAN]
            vel[z0 + k] = frac * here[:, L:] - (crow[z0 + k] + here[:, :L])
        return carry

    lax.fori_loop(0, depth // group_planes, normal_planes, 0)

    def at(z, x0, d):
        return vel[z, pl.ds(EDGE + x0 + d, STEP), :]

    def q_at(f, z, x0, d):
        return uw[f, z, pl.ds(HALO + x0 + d, STEP), :]

    def split(z, left):
        for x0 in range(0, L, STEP):
            v = at(z, x0, 0)
            for f, field in enumerate((q_at(0, z, x0, 0), v, q_at(1, z, x0, 0))):
                left[pl.ds(f * L + x0, STEP), :] = pieces_of_two(field, v * field)

    def plane(z, left, right, later):
        turn = lax.rem(2 * L - 4 - SLOT * lax.rem(z, half), L)
        right[...] = jnp.dot(left[...], weights[...], preferred_element_type=F32)
        if later is not None:
            split(*later)
        for x0 in range(0, L, STEP):
            own = pl.ds(x0, STEP)
            (along_x,) = skew(lambda d: q_at(0, z, x0, d), (lambda d: at(z, x0, d),))
            (along_z,) = skew(lambda d: q_at(1, around(z, d), x0, 0), (lambda d: at(around(z, d), x0, 0),))
            result[z, 1, own, :] = m120[own, :] * along_x + along_z * (1.0 / 120.0)
        for x0 in range(0, L, STEP):
            own = pl.ds(x0, STEP)
            lane = lanes((STEP, L))
            v = at(z, x0, 0)
            for f in range(3):
                others = result[z, 1, own, :] if f == 1 else part[f // 2, z, own, :]
                turned = pltpu.roll(edges[z // half, f, own, :], turn, 1)
                edge = jnp.where((lane < 4) | (lane >= L - 4), turned, 0.0)
                both = right[pl.ds(f * L + x0, STEP), :]
                result[z, f, own, :] = others + (v * both[:, :L] + both[:, L:]) * scale + edge
        pltpu.make_async_copy(result.at[z], out.at[:, z], out_sem.at[z]).start()

    split(0, left_even)

    def two_planes(n, carry):
        z = 2 * n
        plane(z, left_even, right_even, (z + 1, left_odd))
        plane(z + 1, left_odd, right_odd, (around(z, 2), left_even))
        return carry

    lax.fori_loop(0, depth // 2, two_planes, 0)

    def finish(z, carry):
        pltpu.make_async_copy(result.at[z], out.at[:, z], out_sem.at[z]).wait()
        return carry

    lax.fori_loop(0, depth, finish, 0)


STEP = 32
VMEM_FIRST = 24 * 2**20
VMEM_SECOND = 24 * 2**20


def shards(n_gy, velocity, stream_metric, wall_metric):
    depth = velocity.shape[1]
    halves = depth // min(HALF, depth)
    n_ring = len(rings_of(n_gy))
    others = max(size for _, size in rings_of(n_gy)) - 1
    kept = [
        (2, depth, WIDE, L),
        (depth, SPAN, L),
        (3, 2, halves, L, L),
        (3, halves, SPAN, L),
        (2, depth, L, L),
        (3, PACKED, L),
        (ROWS, 8, L),
        (L, L),
    ]
    here = pl.BlockSpec(memory_space=pltpu.VMEM)
    anywhere = pl.BlockSpec(memory_space=pl.ANY)
    dma = pltpu.SemaphoreType.DMA
    held = pl.pallas_call(
        functools.partial(first_kernel, n_gy, depth),
        out_shape=[pltpu.VMEM(shape, F32) for shape in kept],
        in_specs=[pl.BlockSpec(memory_space=pltpu.HBM)] * 3,
        out_specs=[here] * len(kept),
        scratch_shapes=[
            pltpu.VMEM((depth, SPAN, L), F32),
            pltpu.VMEM((WIDE, L), F32),
            pltpu.VMEM((3 * L, 2 * L), BF16),
            pltpu.VMEM((n_ring, PACKED, L), F32),
            pltpu.VMEM((n_ring, others, PACKED, L), F32),
            pltpu.VMEM((2, L), F32),
            pltpu.VMEM((n_gy, L), F32),
            pltpu.VMEM((WIDE, 3 * L), BF16),
            pltpu.VMEM((WIDE, 3 * L), BF16),
            dma((4,)), dma((2, 2)), dma((2, 2)), dma((2, 2)), dma((2, 2)),
            dma((n_ring, others)), dma((n_ring, others)),
        ],
        compiler_params=pltpu.CompilerParams(
            collective_id=0, has_side_effects=True, vmem_limit_bytes=VMEM_FIRST),
        name="exchange",
    )(*(pltpu.with_memory_space_constraint(x, pltpu.HBM)
        for x in (velocity, stream_metric.reshape(2, L), wall_metric.reshape(n_gy, L))))
    return pl.pallas_call(
        functools.partial(second_kernel, depth),
        out_shape=jax.ShapeDtypeStruct((3, depth, L, L), F32),
        in_specs=[here] * len(kept),
        out_specs=anywhere,
        scratch_shapes=[
            pltpu.VMEM((depth, SPAN, L), F32),
            pltpu.VMEM((depth, 3, L, L), F32),
            pltpu.VMEM((3, WIDE, L), F32),
            pltpu.VMEM((2, halves, SPAN, L), F32),
            pltpu.VMEM((halves, 3, L, L), F32),
            pltpu.VMEM((6 * L, 2 * L), BF16),
            pltpu.VMEM((3 * L, 6 * L), BF16),
            pltpu.VMEM((3 * L, 6 * L), BF16),
            pltpu.VMEM((3 * L, 2 * L), F32),
            pltpu.VMEM((3 * L, 2 * L), F32),
            dma((depth,)),
        ],
        compiler_params=pltpu.CompilerParams(vmem_limit_bytes=VMEM_SECOND),
        name="advect",
    )(*held)


def solution(mesh):
    spec = P(None, None, "gx", "gy")
    return jax.shard_map(
        functools.partial(shards, mesh.shape["gy"]), mesh=mesh,
        in_specs=(spec, P(), P()), out_specs=spec, check_vma=False)
```

```python
import functools

import jax
import jax.numpy as jnp
from jax import lax
from jax.experimental import pallas as pl
from jax.experimental.pallas import tpu as pltpu
from jax.sharding import PartitionSpec as P

MESH = pl.DeviceIdType.MESH
F32, BF16 = jnp.float32, jnp.bfloat16
L = 128
HALO = 8
EDGE = 4
WIDE = L + 2 * HALO
SPAN = L + 2 * EDGE
CENTRAL = (45.0, -9.0, 1.0)
INTERIOR = (-1.0, 9.0, -45.0, 0.0, 45.0, -9.0, 1.0)
ROW_FIRST = (0.0, 0.0, 0.0, -110.0, 180.0, -90.0, 20.0)
ROW_SECOND = (0.0, 0.0, -20.0, -30.0, 60.0, -10.0, 0.0)
ROW_THIRD = (0.0, 5.0, -40.0, 0.0, 40.0, -5.0, 0.0)
ROW_SECOND_LAST = (0.0, 10.0, -60.0, 30.0, 20.0, 0.0, 0.0)
ROW_LAST = (-20.0, 90.0, -180.0, 110.0, 0.0, 0.0, 0.0)
TILES = SPAN // 8
GROUPS = -(-TILES // 4)
PACKED = 8 * GROUPS
SLOT, HALF = 8, 16
ROW_FRAC, ROW_SCALE, ROW_OWN, ROW_AWAY, ROW_SLOT, ROW_SLOT_SCALE, ROWS = 7, 8, 9, 10, 11, 18, 19


def rings_of(count):
    size = 4 if count % 4 == 0 and count > 16 else 2
    rings, stride = [], 1
    while stride < count:
        rings.append((stride, size))
        stride *= size
    return rings


def lanes(shape):
    return lax.broadcasted_iota(jnp.int32, shape, len(shape) - 1)


def rolled(x, shift):
    if isinstance(shift, int):
        shift %= L
        if shift == 0:
            return x
    return pltpu.roll(x, shift, len(x.shape) - 1)


def running(x):
    lane = lanes(x.shape)
    step = 1
    while step < L:
        x = x + jnp.where(lane >= step, rolled(x, step), 0.0)
        step *= 2
    return x


def scaled(x, weight):
    return x if weight == 1.0 else x * weight


def chunks(total, size):
    return [(min(i, total - size), size) for i in range(0, total, size)]


def three(x):
    high = x.astype(BF16)
    rest = x - high.astype(F32)
    middle = rest.astype(BF16)
    low = (rest - middle.astype(F32)).astype(BF16)
    return high, middle, low


def pieces(x):
    return jnp.concatenate(three(x), axis=1)


def pieces_of(*arrays):
    return jnp.concatenate([part for same in zip(*map(three, arrays)) for part in same], axis=1)


def skew(adv, fields):
    centre = adv(0)
    sums = [None] * len(fields)
    if len(fields) == 1:
        total = None
        for d, weight in enumerate(CENTRAL, start=1):
            term = (centre + adv(d)) * fields[0](d) - (centre + adv(-d)) * fields[0](-d)
            total = scaled(term, weight) if total is None else total + scaled(term, weight)
        return [total]
    for d, weight in enumerate(CENTRAL, start=1):
        up = scaled(centre + adv(d), weight)
        down = scaled(centre + adv(-d), weight)
        for n, field in enumerate(fields):
            term = up * field(d) - down * field(-d)
            sums[n] = term if sums[n] is None else sums[n] + term
    return sums


def slope_sum(field):
    total = None
    for d, weight in enumerate(CENTRAL, start=1):
        term = scaled(field(d) - field(-d), weight)
        total = term if total is None else total + term
    return total


def store_weights(ref, matrix):
    matrix = matrix.astype(BF16)
    nothing = jnp.zeros((L, L), BF16)
    for n in range(3):
        ref[2 * n * L:(2 * n + 1) * L, :] = jnp.concatenate([matrix, nothing], axis=1)
        ref[(2 * n + 1) * L:(2 * n + 2) * L, :] = jnp.concatenate([nothing, matrix], axis=1)


def first_kernel(
    n_gy, depth,
    vel, sm_far, wm_far,
    uw, crow, halo, shalo, sland, part, lines, rows, m120,
    slope, m_wide, ladder, narrowing, hpack, spack, stage_out, stage_in, sm, wm,
    load_sem, gx_send, gx_recv, y_send, y_recv, st_send, st_recv,
):
    gx, gy = lax.axis_index("gx"), lax.axis_index("gy")
    other = 1 - gx
    rings = rings_of(n_gy)
    up_gy, down_gy = lax.rem(gy + 1, n_gy), lax.rem(gy + n_gy - 1, n_gy)
    half = min(HALF, depth)
    halves = depth // half

    def peer(stride, size, offset):
        place = lax.rem(gy // stride, size)
        return gy + (lax.rem(place + offset, size) - place) * stride

    small = [pltpu.make_async_copy(sm_far, sm, load_sem.at[2]), pltpu.make_async_copy(wm_far, wm, load_sem.at[3])]
    for copy in small:
        copy.start()
    loads = []
    for f in range(2):
        loads.append(pltpu.make_async_copy(vel.at[f], uw.at[f, :, pl.ds(HALO, L)], load_sem.at[f]))
        loads[-1].start()

    barrier = pltpu.get_barrier_semaphore()
    count = 0
    targets = [{"gx": other}, {"gy": up_gy}, {"gy": down_gy}]
    for stride, size in rings:
        targets += [{"gy": peer(stride, size, o)} for o in range(1, size)]
    for target in targets:
        pl.semaphore_signal(barrier, inc=1, device_id=target, device_id_type=MESH)
        count += 1

    for copy in small:
        copy.wait()
    rid = lax.broadcasted_iota(jnp.int32, (n_gy, L), 0)
    wall = wm[...]
    recip = 1.0 / wall

    def row_at(values, index):
        picked = jnp.sum(jnp.where(rid == index, values, 0.0), axis=0, keepdims=True)
        return jnp.broadcast_to(picked, (8, L))

    def whole(values):
        return jnp.sum(jnp.sum(values, axis=0, keepdims=True), axis=1, keepdims=True)

    total_h = whole(recip)
    below_h = whole(jnp.where(rid < gy, recip, 0.0))
    r_own, r_next, r_prev = row_at(recip, gy), row_at(recip, up_gy), row_at(recip, down_gy)
    wall_own = row_at(wall, gy)
    lane8 = lanes((8, L))
    run_own, run_next, run_prev = running(r_own), running(r_next), running(r_prev)
    sum_own = jnp.sum(r_own[0:1], axis=1, keepdims=True)
    sum_prev = jnp.sum(r_prev[0:1], axis=1, keepdims=True)
    frac = (below_h + (run_own - 0.5 * r_own)) / total_h
    frac_next = (below_h + sum_own + (run_next - 0.5 * r_next)) / total_h
    frac_prev = (below_h - sum_prev + (run_prev - 0.5 * r_prev)) / total_h
    scale = wall_own * (1.0 / 120.0)
    rows[ROW_FRAC] = frac
    rows[ROW_SCALE] = scale

    def slots(last, first):
        values = jnp.where(lane8 < 4, rolled(last, 4), 0.0)
        values = values + jnp.where((lane8 >= 4) & (lane8 < 8), rolled(first, 4), 0.0)
        step = SLOT
        while step < L:
            values = values + rolled(values, step)
            step *= 2
        return values

    rows[ROW_OWN] = slots(frac, frac)
    rows[ROW_AWAY] = slots(frac_prev, frac_next)
    place = gy * L + lane8
    last_row = n_gy * L - 1
    for k in range(7):
        entry = jnp.full((8, L), INTERIOR[k], F32)
        for row, table in ((0, ROW_FIRST), (1, ROW_SECOND), (2, ROW_THIRD), (last_row - 2, ROW_THIRD),
                           (last_row - 1, ROW_SECOND_LAST), (last_row, ROW_LAST)):
            entry = jnp.where(place == row, table[k], entry)
        rows[k] = entry
        rows[ROW_SLOT + k] = slots(entry, entry)
    rows[ROW_SLOT_SCALE] = slots(scale, scale)
    r60 = r_own[0:1] * (1.0 / 60.0)

    first_row, second_row = sm[0:1, :], sm[1:2, :]
    own_m = jnp.where(gx == 0, first_row, second_row)
    other_m = jnp.where(gx == 0, second_row, first_row)
    own_cols = jnp.broadcast_to(own_m, (L, L)).T
    other_cols = jnp.broadcast_to(other_m, (L, L)).T
    m_wide[0:HALO, :] = other_cols[L - HALO:L, :]
    m_wide[HALO:HALO + L, :] = own_cols
    m_wide[HALO + L:WIDE, :] = other_cols[0:HALO, :]
    m120[...] = own_cols * (1.0 / 120.0)
    source = lax.broadcasted_iota(jnp.int32, (L, L), 0)
    target = lanes((L, L))
    store_weights(ladder, jnp.where(source < target, 1.0, jnp.where(source == target, 0.5, 0.0)))

    early = (gx == 0) | (gy < n_gy // 8)
    ahead = jnp.where(gy == 0, (5 * depth) // 8, jnp.where((gx == 0) & (gy < n_gy // 2), depth // 4, 0))

    def around(z, d):
        return lax.rem(z + (depth + d), depth)

    def plane_terms(z, starts):
        for x0 in starts:
            size = 16

            def at(f):
                return lambda d: uw[f, z, pl.ds(HALO + x0 + d, size), :]

            def over(f):
                return lambda d: uw[f, around(z, d), pl.ds(HALO + x0, size), :]

            along_x = skew(at(0), (at(0), at(1)))
            along_z = skew(over(1), (over(0), over(1)))
            m = m120[pl.ds(x0, size), :]
            for f in range(2):
                part[f, z, pl.ds(x0, size), :] = m * along_x[f] + along_z[f] * (1.0 / 120.0)

    def inner_terms(z, carry):
        plane_terms(z, range(16, L - 16, 16))
        return carry

    def outer_terms(z, carry):
        plane_terms(z, (0, L - 16))
        return carry

    def send_slots(source, landing, n):
        copies = []
        for side, where in enumerate((down_gy, up_gy)):
            copies.append(pltpu.make_async_remote_copy(
                src_ref=source.at[side], dst_ref=landing.at[side],
                send_sem=y_send.at[n, side], recv_sem=y_recv.at[n, side],
                device_id={"gy": where}, device_id_type=MESH))
            copies[-1].start()
        return copies

    def pack(read, extent):
        slot = lanes((extent, L)) // SLOT
        result = []
        for h in range(halves):
            def body(z, packed):
                return jnp.where(slot == z, pltpu.roll(read(h * half + z), SLOT * z + 4, 1), packed)

            result.append(lax.fori_loop(0, half, body, jnp.zeros((extent, L), F32), unroll=4))
        return result

    def pack_fields():
        for f in range(2):
            both = jnp.dot(pieces_of(*pack(lambda z, f=f: uw[f, z, pl.ds(HALO, L), :], L)), narrowing[...],
                           preferred_element_type=F32)
            for side in range(2):
                hpack[side, f] = both[:, side * L:(side + 1) * L]

    from_row = lax.broadcasted_iota(jnp.int32, (halves * L, 2 * L), 0)
    to_lane = lanes((halves * L, 2 * L))
    lane, place8 = lax.rem(from_row, L), lax.rem(from_row, SLOT)
    plane_lane = 4 * (half * (from_row // L) + lane // SLOT)
    narrow = ((place8 >= 4) & (to_lane == plane_lane + place8 - 4)) | ((place8 < 4) & (to_lane == L + plane_lane + place8))
    narrow = narrow.astype(F32).astype(BF16)
    for n in range(3):
        narrowing[n * halves * L:(n + 1) * halves * L, :] = narrow

    for copy in loads:
        copy.wait()
    pl.when(early)(pack_fields)
    lax.fori_loop(0, ahead, inner_terms, 0)

    pl.semaphore_wait(barrier, count)

    gx_copies = []
    for f in range(2):
        for side, (src, dst) in enumerate(((L - HALO, 0), (0, HALO + L))):
            gx_copies.append(pltpu.make_async_remote_copy(
                src_ref=vel.at[f, :, pl.ds(src, HALO)], dst_ref=uw.at[f, :, pl.ds(dst, HALO)],
                send_sem=gx_send.at[f, side], recv_sem=gx_recv.at[f, side],
                device_id={"gx": other}, device_id_type=MESH))
            gx_copies[-1].start()

    for copy in gx_copies:
        copy.wait()

    lane_small = lanes((8, L))
    shift = HALO - EDGE

    def slope_plane(z, sums):
        sums = list(sums)
        for x0, size in chunks(SPAN, 8):
            du = slope_sum(lambda d: uw[0, z, pl.ds(shift + x0 + d, size), :])
            dw = slope_sum(lambda d: uw[1, around(z, d), pl.ds(shift + x0, size), :])
            value = (m_wide[pl.ds(shift + x0, size), :] * du + dw) * r60
            slope[z, pl.ds(x0, size), :] = value
            group, quarter = x0 // 32, (x0 // 8) % 4
            line = jnp.sum(value, axis=1, keepdims=True)
            sums[group] = jnp.where(lane_small == 32 * quarter + z, line, sums[group])
        return tuple(sums)

    sums = lax.fori_loop(0, depth, slope_plane, tuple(jnp.zeros((8, L), F32) for _ in range(GROUPS)), unroll=2)
    own = jnp.concatenate(sums, axis=0)
    lines[2] = own

    def send_stage(stage):
        stride, size = rings[stage]
        copies = []
        for o in range(1, size):
            copies.append(pltpu.make_async_remote_copy(
                src_ref=stage_out.at[stage], dst_ref=stage_in.at[stage, o - 1],
                send_sem=st_send.at[stage, o - 1], recv_sem=st_recv.at[stage, o - 1],
                device_id={"gy": peer(stride, size, o)}, device_id_type=MESH))
            copies[-1].start()
        return copies

    def climb(n, carry):
        z = 2 * n
        climbed = jnp.dot(pieces_of(slope[z], slope[z + 1]), ladder[...], preferred_element_type=F32)
        crow[z] = climbed[:, :L]
        crow[z + 1] = climbed[:, L:]
        return carry

    y_copies = []

    def work(stage):
        if stage == 0:
            pl.when(jnp.logical_not(early))(pack_fields)
            y_copies.extend(send_slots(hpack, halo, 0))

            for h, value in enumerate(pack(lambda z: slope[z], SPAN)):
                shalo[h] = value
            both = jnp.dot(pieces_of(*(shalo[h] for h in range(halves))), narrowing[...], preferred_element_type=F32)
            for side in range(2):
                spack[side] = both[:, side * L:(side + 1) * L]
            y_copies.extend(send_slots(spack, sland, 1))
        if stage == 1 % len(rings):
            lax.fori_loop(0, depth // 2, climb, 0)
        if stage == len(rings) - 1:
            lax.fori_loop(0, depth, outer_terms, 0)

    below = jnp.zeros((PACKED, L), F32)
    for stage, (stride, size) in enumerate(rings):
        stage_out[stage] = own
        copies = send_stage(stage)
        work(stage)
        mine = lax.rem(gy // stride, size)
        for copy in copies:
            copy.wait()
        own = stage_out[stage]
        for o in range(1, size):
            sender = lax.rem(mine + size - o, size)
            value = stage_in[stage, o - 1]
            own = own + value
            below = below + jnp.where(sender < mine, value, 0.0)
        if stage < len(rings) - 1:
            lines[0] = below
            below = lines[0]
    lines[0] = below
    lines[1] = own
    lax.fori_loop(ahead, depth, inner_terms, 0)

    for copy in y_copies:
        copy.wait()


def second_kernel(
    depth, uw, crow, halo, shalo, sland, part, lines, rows, m120,
    out, vel, result, parts, vslots, edges, weights, widening, hwide,
    left_even, left_odd, right_even, right_odd, out_sem,
):
    half = min(HALF, depth)
    halves = depth // half
    frac = rows[ROW_FRAC][0:1]
    scale = rows[ROW_SCALE][0:1]

    def around(z, d):
        return lax.rem(z + (depth + d), depth)

    source = lax.broadcasted_iota(jnp.int32, (L, L), 0)
    target = lanes((L, L))

    packed = pieces(lines[...].reshape(3 * PACKED, L))
    from_lane = lax.broadcasted_iota(jnp.int32, (3 * L, L), 0)
    to_lane = lanes((3 * L, L))
    for quarter in range(4):
        pick = (from_lane // L == to_lane // 32) & (lax.rem(from_lane, L) == 32 * quarter + lax.rem(to_lane, 32))
        found = jnp.dot(packed, pick.astype(F32).astype(BF16), preferred_element_type=F32)
        for group in range(GROUPS):
            tile = 4 * group + quarter
            if tile < TILES:
                for n in range(3):
                    at = n * PACKED + 8 * group
                    parts[n, pl.ds(8 * tile, 8), :] = found[at:at + 8]
    for n in range(3):
        parts[n, pl.ds(SPAN, 8), :] = jnp.zeros((8, L), F32)
    source2 = lax.broadcasted_iota(jnp.int32, (L, halves * L), 0)
    target2 = lanes((L, halves * L))
    to_slot = (lax.rem(source2, 32) == half * (target2 // L) + lax.rem(target2, L) // SLOT) & (source2 < 96)
    to_slot = to_slot.astype(F32).astype(BF16)

    same_slot = source // SLOT == target // SLOT
    place, aim = lax.rem(source, SLOT), lax.rem(target, SLOT)
    passed = ((place >= 4) & (place < aim)) | ((place < 4) & (place > aim))
    same_side = same_slot & ((place >= 4) == (aim >= 4))
    local = jnp.where(same_side & passed, 1.0, jnp.where(source == target, 0.5, 0.0)).astype(BF16)
    local = jnp.concatenate([local, local, local], axis=0)
    first_rows = lax.rem(lanes((SPAN, L)), SLOT) >= 4
    from_row = lax.broadcasted_iota(jnp.int32, (2 * L, halves * L), 0)
    to_lane = lanes((2 * L, halves * L))
    place8 = lax.rem(to_lane, SLOT)
    plane_lane = 4 * (half * (to_lane // L) + lax.rem(to_lane, L) // SLOT)
    widen = ((place8 >= 4) & (from_row == plane_lane + place8 - 4)) | ((place8 < 4) & (from_row == L + plane_lane + place8))
    widen = widen.astype(F32).astype(BF16)
    for n in range(3):
        widening[2 * n * L:2 * (n + 1) * L, :] = widen

    def widened(first, last):
        return jnp.dot(pieces_of(first, last), widening[...], preferred_element_type=F32)

    for f in range(2):
        wide = widened(halo[0, f], halo[1, f])
        for h in range(halves):
            hwide[h, f] = wide[:, h * L:(h + 1) * L]
    swide = widened(sland[0], sland[1])
    spread = [jnp.dot(parts[n].astype(BF16), to_slot, preferred_element_type=F32) for n in range(3)]
    for h in range(halves):
        below, total, line = (x[:SPAN, h * L:(h + 1) * L] for x in spread)
        near = jnp.dot(pieces(shalo[h]), local, preferred_element_type=F32)
        away = jnp.dot(pieces(swide[:, h * L:(h + 1) * L]), local, preferred_element_type=F32)
        near = jnp.where(first_rows, near, line - near)
        away = jnp.where(first_rows, line + away, -away)
        vslots[0, h] = rows[ROW_OWN][0:1] * total - (near + below)
        vslots[1, h] = rows[ROW_AWAY][0:1] * total - (away + below)

    across = same_slot & ((place >= 4) != (aim >= 4))
    stencil = jnp.zeros((L, L), F32)
    for k in range(7):
        stencil = jnp.where(across & (source - target == k - 3), rows[ROW_SLOT + k][0:1], stencil)
    store_weights(weights, stencil)
    scale8 = rows[ROW_SLOT_SCALE][0:1]
    for h in range(halves):
        for x0, size in chunks(L, 32):
            area = pl.ds(x0, size)
            v = vslots[1, h, pl.ds(EDGE + x0, size), :]
            for f, field in enumerate((hwide[h, 0, area, :], v, hwide[h, 1, area, :])):
                left_even[pl.ds(f * L + x0, size), :] = pieces_of(field, v * field)
        right_even[...] = jnp.dot(left_even[...], weights[...], preferred_element_type=F32)
        for x0, size in chunks(L, 32):
            v = vslots[0, h, pl.ds(EDGE + x0, size), :]
            for f in range(3):
                both = right_even[pl.ds(f * L + x0, size), :]
                edges[h, f, pl.ds(x0, size), :] = (v * both[:, :L] + both[:, L:]) * scale8

    stencil = jnp.zeros((L, L), F32)
    for k in range(7):
        stencil = jnp.where(source - target == k - 3, rows[k][0:1], stencil)
    store_weights(weights, stencil)

    source3 = lax.broadcasted_iota(jnp.int32, (2 * L, 2 * L), 0)
    target3 = lanes((2 * L, 2 * L))
    ones = (source3 // L == target3 // L).astype(F32).astype(BF16)
    both = jnp.concatenate([parts[0], parts[1]], axis=1)
    plane_of = lax.rem(lanes((WIDE, 2 * L)), 32)
    group_planes = 4

    def normal_planes(n, carry):
        z0 = group_planes * n
        chosen = [jnp.where(plane_of == z0 + k, both, 0.0).astype(BF16) for k in range(group_planes)]
        found = jnp.dot(jnp.concatenate(chosen, axis=0), ones, preferred_element_type=F32)
        for k in range(group_planes):
            here = found[k * WIDE:k * WIDE + SPAN]
            vel[z0 + k] = frac * here[:, L:] - (crow[z0 + k] + here[:, :L])
        return carry

    lax.fori_loop(0, depth // group_planes, normal_planes, 0)

    def at(z, x0, d):
        return vel[z, pl.ds(EDGE + x0 + d, STEP), :]

    def q_at(f, z, x0, d):
        return uw[f, z, pl.ds(HALO + x0 + d, STEP), :]

    def split(z, left):
        for x0 in range(0, L, STEP):
            v = at(z, x0, 0)
            for f, field in enumerate((q_at(0, z, x0, 0), v, q_at(1, z, x0, 0))):
                left[pl.ds(f * L + x0, STEP), :] = pieces_of(field, v * field)

    def plane(z, left, right, later):
        turn = lax.rem(2 * L - 4 - SLOT * lax.rem(z, half), L)
        right[...] = jnp.dot(left[...], weights[...], preferred_element_type=F32)
        if later is not None:
            split(*later)
        for x0 in range(0, L, STEP):
            own = pl.ds(x0, STEP)
            (along_x,) = skew(lambda d: q_at(0, z, x0, d), (lambda d: at(z, x0, d),))
            (along_z,) = skew(lambda d: q_at(1, around(z, d), x0, 0), (lambda d: at(around(z, d), x0, 0),))
            result[z, 1, own, :] = m120[own, :] * along_x + along_z * (1.0 / 120.0)
        for x0 in range(0, L, STEP):
            own = pl.ds(x0, STEP)
            lane = lanes((STEP, L))
            v = at(z, x0, 0)
            for f in range(3):
                others = result[z, 1, own, :] if f == 1 else part[f // 2, z, own, :]
                turned = pltpu.roll(edges[z // half, f, own, :], turn, 1)
                edge = jnp.where((lane < 4) | (lane >= L - 4), turned, 0.0)
                both = right[pl.ds(f * L + x0, STEP), :]
                result[z, f, own, :] = others + (v * both[:, :L] + both[:, L:]) * scale + edge
        pltpu.make_async_copy(result.at[z], out.at[:, z], out_sem.at[z]).start()

    split(0, left_even)

    def two_planes(n, carry):
        z = 2 * n
        plane(z, left_even, right_even, (z + 1, left_odd))
        plane(z + 1, left_odd, right_odd, (around(z, 2), left_even))
        return carry

    lax.fori_loop(0, depth // 2, two_planes, 0)

    def finish(z, carry):
        pltpu.make_async_copy(result.at[z], out.at[:, z], out_sem.at[z]).wait()
        return carry

    lax.fori_loop(0, depth, finish, 0)


STEP = 32
VMEM_FIRST = 24 * 2**20
VMEM_SECOND = 24 * 2**20


def shards(n_gy, velocity, stream_metric, wall_metric):
    depth = velocity.shape[1]
    halves = depth // min(HALF, depth)
    n_ring = len(rings_of(n_gy))
    others = max(size for _, size in rings_of(n_gy)) - 1
    kept = [
        (2, depth, WIDE, L),
        (depth, SPAN, L),
        (2, 2, L, L),
        (halves, SPAN, L),
        (2, SPAN, L),
        (2, depth, L, L),
        (3, PACKED, L),
        (ROWS, 8, L),
        (L, L),
    ]
    here = pl.BlockSpec(memory_space=pltpu.VMEM)
    anywhere = pl.BlockSpec(memory_space=pl.ANY)
    dma = pltpu.SemaphoreType.DMA
    held = pl.pallas_call(
        functools.partial(first_kernel, n_gy, depth),
        out_shape=[pltpu.VMEM(shape, F32) for shape in kept],
        in_specs=[pl.BlockSpec(memory_space=pltpu.HBM)] * 3,
        out_specs=[here] * len(kept),
        scratch_shapes=[
            pltpu.VMEM((depth, SPAN, L), F32),
            pltpu.VMEM((WIDE, L), F32),
            pltpu.VMEM((6 * L, 2 * L), BF16),
            pltpu.VMEM((3 * halves * L, 2 * L), BF16),
            pltpu.VMEM((2, 2, L, L), F32),
            pltpu.VMEM((2, SPAN, L), F32),
            pltpu.VMEM((n_ring, PACKED, L), F32),
            pltpu.VMEM((n_ring, others, PACKED, L), F32),
            pltpu.VMEM((2, L), F32),
            pltpu.VMEM((n_gy, L), F32),
            dma((4,)), dma((2, 2)), dma((2, 2)), dma((2, 2)), dma((2, 2)),
            dma((n_ring, others)), dma((n_ring, others)),
        ],
        compiler_params=pltpu.CompilerParams(
            collective_id=0, has_side_effects=True, vmem_limit_bytes=VMEM_FIRST),
        name="exchange",
    )(*(pltpu.with_memory_space_constraint(x, pltpu.HBM)
        for x in (velocity, stream_metric.reshape(2, L), wall_metric.reshape(n_gy, L))))
    return pl.pallas_call(
        functools.partial(second_kernel, depth),
        out_shape=jax.ShapeDtypeStruct((3, depth, L, L), F32),
        in_specs=[here] * len(kept),
        out_specs=anywhere,
        scratch_shapes=[
            pltpu.VMEM((depth, SPAN, L), F32),
            pltpu.VMEM((depth, 3, L, L), F32),
            pltpu.VMEM((3, WIDE, L), F32),
            pltpu.VMEM((2, halves, SPAN, L), F32),
            pltpu.VMEM((halves, 3, L, L), F32),
            pltpu.VMEM((6 * L, 2 * L), BF16),
            pltpu.VMEM((6 * L, halves * L), BF16),
            pltpu.VMEM((halves, 2, L, L), F32),
            pltpu.VMEM((3 * L, 6 * L), BF16),
            pltpu.VMEM((3 * L, 6 * L), BF16),
            pltpu.VMEM((3 * L, 2 * L), F32),
            pltpu.VMEM((3 * L, 2 * L), F32),
            dma((depth,)),
        ],
        compiler_params=pltpu.CompilerParams(vmem_limit_bytes=VMEM_SECOND),
        name="advect",
    )(*held)


def solution(mesh):
    spec = P(None, None, "gx", "gy")
    return jax.shard_map(
        functools.partial(shards, mesh.shape["gy"]), mesh=mesh,
        in_specs=(spec, P(), P()), out_specs=spec, check_vma=False)
```

```python
import functools

import jax
import jax.numpy as jnp
from jax import lax
from jax.experimental import pallas as pl
from jax.experimental.pallas import tpu as pltpu
from jax.sharding import PartitionSpec as P

MESH = pl.DeviceIdType.MESH
F32, BF16 = jnp.float32, jnp.bfloat16
L = 128
HALO = 8
EDGE = 4
WIDE = L + 2 * HALO
SPAN = L + 2 * EDGE
CENTRAL = (45.0, -9.0, 1.0)
INTERIOR = (-1.0, 9.0, -45.0, 0.0, 45.0, -9.0, 1.0)
ROW_FIRST = (0.0, 0.0, 0.0, -110.0, 180.0, -90.0, 20.0)
ROW_SECOND = (0.0, 0.0, -20.0, -30.0, 60.0, -10.0, 0.0)
ROW_THIRD = (0.0, 5.0, -40.0, 0.0, 40.0, -5.0, 0.0)
ROW_SECOND_LAST = (0.0, 10.0, -60.0, 30.0, 20.0, 0.0, 0.0)
ROW_LAST = (-20.0, 90.0, -180.0, 110.0, 0.0, 0.0, 0.0)
TILES = SPAN // 8
GROUPS = -(-TILES // 4)
PACKED = 8 * GROUPS
SLOT, HALF = 8, 16
ROW_FRAC, ROW_SCALE, ROW_OWN, ROW_AWAY, ROW_SLOT, ROW_SLOT_SCALE, ROWS = 7, 8, 9, 10, 11, 18, 19


def rings_of(count):
    size = 4 if count % 4 == 0 and count > 16 else 2
    rings, stride = [], 1
    while stride < count:
        rings.append((stride, size))
        stride *= size
    return rings


def lanes(shape):
    return lax.broadcasted_iota(jnp.int32, shape, len(shape) - 1)


def rolled(x, shift):
    if isinstance(shift, int):
        shift %= L
        if shift == 0:
            return x
    return pltpu.roll(x, shift, len(x.shape) - 1)


def running(x):
    lane = lanes(x.shape)
    step = 1
    while step < L:
        x = x + jnp.where(lane >= step, rolled(x, step), 0.0)
        step *= 2
    return x


def scaled(x, weight):
    return x if weight == 1.0 else x * weight


def chunks(total, size):
    return [(min(i, total - size), size) for i in range(0, total, size)]


def three(x):
    high = x.astype(BF16)
    rest = x - high.astype(F32)
    middle = rest.astype(BF16)
    low = (rest - middle.astype(F32)).astype(BF16)
    return high, middle, low


def pieces(x):
    return jnp.concatenate(three(x), axis=1)


def pieces_of(*arrays):
    return jnp.concatenate([part for same in zip(*map(three, arrays)) for part in same], axis=1)


def skew(adv, fields):
    centre = adv(0)
    sums = [None] * len(fields)
    if len(fields) == 1:
        total = None
        for d, weight in enumerate(CENTRAL, start=1):
            term = (centre + adv(d)) * fields[0](d) - (centre + adv(-d)) * fields[0](-d)
            total = scaled(term, weight) if total is None else total + scaled(term, weight)
        return [total]
    for d, weight in enumerate(CENTRAL, start=1):
        up = scaled(centre + adv(d), weight)
        down = scaled(centre + adv(-d), weight)
        for n, field in enumerate(fields):
            term = up * field(d) - down * field(-d)
            sums[n] = term if sums[n] is None else sums[n] + term
    return sums


def slope_sum(field):
    total = None
    for d, weight in enumerate(CENTRAL, start=1):
        term = scaled(field(d) - field(-d), weight)
        total = term if total is None else total + term
    return total


def store_weights(ref, matrix):
    matrix = matrix.astype(BF16)
    nothing = jnp.zeros((L, L), BF16)
    for n in range(3):
        ref[2 * n * L:(2 * n + 1) * L, :] = jnp.concatenate([matrix, nothing], axis=1)
        ref[(2 * n + 1) * L:(2 * n + 2) * L, :] = jnp.concatenate([nothing, matrix], axis=1)


def first_kernel(
    n_gy, depth,
    vel, sm_far, wm_far,
    uw, crow, halo, shalo, sland, part, lines, rows, m120,
    slope, m_wide, ladder, narrowing, hpack, spack, stage_out, stage_in, sm, wm, left_even, left_odd,
    load_sem, gx_send, gx_recv, y_send, y_recv, st_send, st_recv,
):
    gx, gy = lax.axis_index("gx"), lax.axis_index("gy")
    other = 1 - gx
    rings = rings_of(n_gy)
    up_gy, down_gy = lax.rem(gy + 1, n_gy), lax.rem(gy + n_gy - 1, n_gy)
    half = min(HALF, depth)
    halves = depth // half

    def peer(stride, size, offset):
        place = lax.rem(gy // stride, size)
        return gy + (lax.rem(place + offset, size) - place) * stride

    small = [pltpu.make_async_copy(sm_far, sm, load_sem.at[2]), pltpu.make_async_copy(wm_far, wm, load_sem.at[3])]
    for copy in small:
        copy.start()
    loads = []
    for f in range(2):
        loads.append(pltpu.make_async_copy(vel.at[f], uw.at[f, :, pl.ds(HALO, L)], load_sem.at[f]))
        loads[-1].start()

    barrier = pltpu.get_barrier_semaphore()
    count = 0
    targets = [{"gx": other}, {"gy": up_gy}, {"gy": down_gy}]
    for stride, size in rings:
        targets += [{"gy": peer(stride, size, o)} for o in range(1, size)]
    for target in targets:
        pl.semaphore_signal(barrier, inc=1, device_id=target, device_id_type=MESH)
        count += 1

    for copy in small:
        copy.wait()
    rid = lax.broadcasted_iota(jnp.int32, (n_gy, L), 0)
    wall = wm[...]
    recip = 1.0 / wall

    def row_at(values, index):
        picked = jnp.sum(jnp.where(rid == index, values, 0.0), axis=0, keepdims=True)
        return jnp.broadcast_to(picked, (8, L))

    def whole(values):
        return jnp.sum(jnp.sum(values, axis=0, keepdims=True), axis=1, keepdims=True)

    total_h = whole(recip)
    below_h = whole(jnp.where(rid < gy, recip, 0.0))
    r_own, r_next, r_prev = row_at(recip, gy), row_at(recip, up_gy), row_at(recip, down_gy)
    wall_own = row_at(wall, gy)
    lane8 = lanes((8, L))
    run_own, run_next, run_prev = running(r_own), running(r_next), running(r_prev)
    sum_own = jnp.sum(r_own[0:1], axis=1, keepdims=True)
    sum_prev = jnp.sum(r_prev[0:1], axis=1, keepdims=True)
    frac = (below_h + (run_own - 0.5 * r_own)) / total_h
    frac_next = (below_h + sum_own + (run_next - 0.5 * r_next)) / total_h
    frac_prev = (below_h - sum_prev + (run_prev - 0.5 * r_prev)) / total_h
    scale = wall_own * (1.0 / 120.0)
    rows[ROW_FRAC] = frac
    rows[ROW_SCALE] = scale

    def slots(last, first):
        values = jnp.where(lane8 < 4, rolled(last, 4), 0.0)
        values = values + jnp.where((lane8 >= 4) & (lane8 < 8), rolled(first, 4), 0.0)
        step = SLOT
        while step < L:
            values = values + rolled(values, step)
            step *= 2
        return values

    rows[ROW_OWN] = slots(frac, frac)
    rows[ROW_AWAY] = slots(frac_prev, frac_next)
    place = gy * L + lane8
    last_row = n_gy * L - 1
    for k in range(7):
        entry = jnp.full((8, L), INTERIOR[k], F32)
        for row, table in ((0, ROW_FIRST), (1, ROW_SECOND), (2, ROW_THIRD), (last_row - 2, ROW_THIRD),
                           (last_row - 1, ROW_SECOND_LAST), (last_row, ROW_LAST)):
            entry = jnp.where(place == row, table[k], entry)
        rows[k] = entry
        rows[ROW_SLOT + k] = slots(entry, entry)
    rows[ROW_SLOT_SCALE] = slots(scale, scale)
    r60 = r_own[0:1] * (1.0 / 60.0)

    first_row, second_row = sm[0:1, :], sm[1:2, :]
    own_m = jnp.where(gx == 0, first_row, second_row)
    other_m = jnp.where(gx == 0, second_row, first_row)
    own_cols = jnp.broadcast_to(own_m, (L, L)).T
    other_cols = jnp.broadcast_to(other_m, (L, L)).T
    m_wide[0:HALO, :] = other_cols[L - HALO:L, :]
    m_wide[HALO:HALO + L, :] = own_cols
    m_wide[HALO + L:WIDE, :] = other_cols[0:HALO, :]
    m120[...] = own_cols * (1.0 / 120.0)
    source = lax.broadcasted_iota(jnp.int32, (L, 2 * L), 0)
    target = lanes((L, 2 * L))
    steps = jnp.where(source < target, 1.0, jnp.where(source == target, 0.5, 0.0)).astype(BF16)
    for n in range(3):
        ladder[n * L:(n + 1) * L, :] = steps


    def around(z, d):
        return lax.rem(z + (depth + d), depth)

    def plane_terms(z, starts):
        for x0 in starts:
            size = 16

            def at(f):
                return lambda d: uw[f, z, pl.ds(HALO + x0 + d, size), :]

            def over(f):
                return lambda d: uw[f, around(z, d), pl.ds(HALO + x0, size), :]

            along_x = skew(at(0), (at(0), at(1)))
            along_z = skew(over(1), (over(0), over(1)))
            m = m120[pl.ds(x0, size), :]
            for f in range(2):
                part[f, z, pl.ds(x0, size), :] = m * along_x[f] + along_z[f] * (1.0 / 120.0)

    def inner_terms(z, carry):
        plane_terms(z, range(0, L, 16))
        return carry

    def send_slots(source, landing, n):
        copies = []
        for side, where in enumerate((down_gy, up_gy)):
            copies.append(pltpu.make_async_remote_copy(
                src_ref=source.at[side], dst_ref=landing.at[side],
                send_sem=y_send.at[n, side], recv_sem=y_recv.at[n, side],
                device_id={"gy": where}, device_id_type=MESH))
            copies[-1].start()
        return copies

    def pack(read, extent):
        slot = lanes((extent, L)) // SLOT
        result = []
        for h in range(halves):
            def body(z, packed):
                return jnp.where(slot == z, pltpu.roll(read(h * half + z), SLOT * z + 4, 1), packed)

            result.append(lax.fori_loop(0, half, body, jnp.zeros((extent, L), F32), unroll=4))
        return result

    def pack_fields():
        for f in range(2):
            both = jnp.dot(pieces_of(*pack(lambda z, f=f: uw[f, z, pl.ds(HALO, L), :], L)), narrowing[...],
                           preferred_element_type=F32)
            for side in range(2):
                hpack[side, f] = both[:, side * L:(side + 1) * L]

    from_row = lax.broadcasted_iota(jnp.int32, (halves * L, 2 * L), 0)
    to_lane = lanes((halves * L, 2 * L))
    lane, place8 = lax.rem(from_row, L), lax.rem(from_row, SLOT)
    plane_lane = 4 * (half * (from_row // L) + lane // SLOT)
    narrow = ((place8 >= 4) & (to_lane == plane_lane + place8 - 4)) | ((place8 < 4) & (to_lane == L + plane_lane + place8))
    narrow = narrow.astype(F32).astype(BF16)
    for n in range(3):
        narrowing[n * halves * L:(n + 1) * halves * L, :] = narrow

    for copy in loads:
        copy.wait()

    pl.semaphore_wait(barrier, count)

    gx_copies = []
    for f in range(2):
        for side, (src, dst) in enumerate(((L - HALO, 0), (0, HALO + L))):
            gx_copies.append(pltpu.make_async_remote_copy(
                src_ref=vel.at[f, :, pl.ds(src, HALO)], dst_ref=uw.at[f, :, pl.ds(dst, HALO)],
                send_sem=gx_send.at[f, side], recv_sem=gx_recv.at[f, side],
                device_id={"gx": other}, device_id_type=MESH))
            gx_copies[-1].start()

    pack_fields()
    y_copies = send_slots(hpack, halo, 0)

    for copy in gx_copies:
        copy.wait()

    lane_small = lanes((8, L))
    shift = HALO - EDGE

    def slope_split(z, left):
        for x0, size in chunks(SPAN, 48):
            du = slope_sum(lambda d: uw[0, z, pl.ds(shift + x0 + d, size), :])
            dw = slope_sum(lambda d: uw[1, around(z, d), pl.ds(shift + x0, size), :])
            value = (m_wide[pl.ds(shift + x0, size), :] * du + dw) * r60
            slope[z, pl.ds(x0, size), :] = value
            left[pl.ds(min(x0, SPAN - size) + (SLOT if x0 + size == SPAN else 0), size), :] = pieces(value)

    def row_in_left(row):
        return row if row < SPAN - 48 else row + SLOT

    def slope_climb(z, left, sums, later):
        climbed = jnp.dot(left[...], ladder[...], preferred_element_type=F32)
        slope_split(*later)
        for tile in range(TILES):
            row = row_in_left(8 * tile)
            crow[z, pl.ds(8 * tile, 8), :] = climbed[row:row + 8, :L]
            group, quarter = tile // 4, tile % 4
            sums[group] = jnp.where(lane_small == 32 * quarter + z, climbed[row:row + 8, L:], sums[group])
        return sums

    slope_split(0, left_even)

    def slope_plane(n, sums):
        z = 2 * n
        sums = slope_climb(z, left_even, list(sums), (z + 1, left_odd))
        return tuple(slope_climb(z + 1, left_odd, sums, (around(z, 2), left_even)))

    sums = lax.fori_loop(0, depth // 2, slope_plane, tuple(jnp.zeros((8, L), F32) for _ in range(GROUPS)))
    own = jnp.concatenate(sums, axis=0)
    lines[2] = own

    def send_stage(stage):
        stride, size = rings[stage]
        copies = []
        for o in range(1, size):
            copies.append(pltpu.make_async_remote_copy(
                src_ref=stage_out.at[stage], dst_ref=stage_in.at[stage, o - 1],
                send_sem=st_send.at[stage, o - 1], recv_sem=st_recv.at[stage, o - 1],
                device_id={"gy": peer(stride, size, o)}, device_id_type=MESH))
            copies[-1].start()
        return copies

    first_cut, second_cut = ((depth * k) // 32 for k in (8, 20))

    def work(stage):
        if stage == 0:
            for h, value in enumerate(pack(lambda z: slope[z], SPAN)):
                shalo[h] = value
            both = jnp.dot(pieces_of(*(shalo[h] for h in range(halves))), narrowing[...], preferred_element_type=F32)
            for side in range(2):
                spack[side] = both[:, side * L:(side + 1) * L]
            y_copies.extend(send_slots(spack, sland, 1))
            lax.fori_loop(0, first_cut, inner_terms, 0)
        if stage == 1 % len(rings):
            lax.fori_loop(first_cut, second_cut, inner_terms, 0)
        if stage == len(rings) - 1:
            lax.fori_loop(second_cut, depth, inner_terms, 0)

    below = jnp.zeros((PACKED, L), F32)
    for stage, (stride, size) in enumerate(rings):
        stage_out[stage] = own
        copies = send_stage(stage)
        work(stage)
        mine = lax.rem(gy // stride, size)
        for copy in copies:
            copy.wait()
        own = stage_out[stage]
        for o in range(1, size):
            sender = lax.rem(mine + size - o, size)
            value = stage_in[stage, o - 1]
            own = own + value
            below = below + jnp.where(sender < mine, value, 0.0)
        if stage < len(rings) - 1:
            lines[0] = below
            below = lines[0]
    lines[0] = below
    lines[1] = own
    for copy in y_copies:
        copy.wait()


def second_kernel(
    depth, uw, crow, halo, shalo, sland, part, lines, rows, m120,
    out, vel, result, parts, vslots, edges, weights, widening, hwide,
    left_even, left_odd, right_even, right_odd, out_sem,
):
    half = min(HALF, depth)
    halves = depth // half
    frac = rows[ROW_FRAC][0:1]
    scale = rows[ROW_SCALE][0:1]

    def around(z, d):
        return lax.rem(z + (depth + d), depth)

    source = lax.broadcasted_iota(jnp.int32, (L, L), 0)
    target = lanes((L, L))

    packed = pieces(lines[...].reshape(3 * PACKED, L))
    from_lane = lax.broadcasted_iota(jnp.int32, (3 * L, L), 0)
    to_lane = lanes((3 * L, L))
    for quarter in range(4):
        pick = (from_lane // L == to_lane // 32) & (lax.rem(from_lane, L) == 32 * quarter + lax.rem(to_lane, 32))
        found = jnp.dot(packed, pick.astype(F32).astype(BF16), preferred_element_type=F32)
        for group in range(GROUPS):
            tile = 4 * group + quarter
            if tile < TILES:
                for n in range(3):
                    at = n * PACKED + 8 * group
                    parts[n, pl.ds(8 * tile, 8), :] = found[at:at + 8]
    for n in range(3):
        parts[n, pl.ds(SPAN, 8), :] = jnp.zeros((8, L), F32)
    source2 = lax.broadcasted_iota(jnp.int32, (L, halves * L), 0)
    target2 = lanes((L, halves * L))
    to_slot = (lax.rem(source2, 32) == half * (target2 // L) + lax.rem(target2, L) // SLOT) & (source2 < 96)
    to_slot = to_slot.astype(F32).astype(BF16)

    same_slot = source // SLOT == target // SLOT
    place, aim = lax.rem(source, SLOT), lax.rem(target, SLOT)
    passed = ((place >= 4) & (place < aim)) | ((place < 4) & (place > aim))
    same_side = same_slot & ((place >= 4) == (aim >= 4))
    local = jnp.where(same_side & passed, 1.0, jnp.where(source == target, 0.5, 0.0)).astype(BF16)
    local = jnp.concatenate([local, local, local], axis=0)
    first_rows = lax.rem(lanes((SPAN, L)), SLOT) >= 4
    from_row = lax.broadcasted_iota(jnp.int32, (2 * L, halves * L), 0)
    to_lane = lanes((2 * L, halves * L))
    place8 = lax.rem(to_lane, SLOT)
    plane_lane = 4 * (half * (to_lane // L) + lax.rem(to_lane, L) // SLOT)
    widen = ((place8 >= 4) & (from_row == plane_lane + place8 - 4)) | ((place8 < 4) & (from_row == L + plane_lane + place8))
    widen = widen.astype(F32).astype(BF16)
    for n in range(3):
        widening[2 * n * L:2 * (n + 1) * L, :] = widen

    def widened(first, last):
        return jnp.dot(pieces_of(first, last), widening[...], preferred_element_type=F32)

    for f in range(2):
        wide = widened(halo[0, f], halo[1, f])
        for h in range(halves):
            hwide[h, f] = wide[:, h * L:(h + 1) * L]
    swide = widened(sland[0], sland[1])
    spread = [jnp.dot(parts[n].astype(BF16), to_slot, preferred_element_type=F32) for n in range(3)]
    for h in range(halves):
        below, total, line = (x[:SPAN, h * L:(h + 1) * L] for x in spread)
        near = jnp.dot(pieces(shalo[h]), local, preferred_element_type=F32)
        away = jnp.dot(pieces(swide[:, h * L:(h + 1) * L]), local, preferred_element_type=F32)
        near = jnp.where(first_rows, near, line - near)
        away = jnp.where(first_rows, line + away, -away)
        vslots[0, h] = rows[ROW_OWN][0:1] * total - (near + below)
        vslots[1, h] = rows[ROW_AWAY][0:1] * total - (away + below)

    across = same_slot & ((place >= 4) != (aim >= 4))
    stencil = jnp.zeros((L, L), F32)
    for k in range(7):
        stencil = jnp.where(across & (source - target == k - 3), rows[ROW_SLOT + k][0:1], stencil)
    store_weights(weights, stencil)
    scale8 = rows[ROW_SLOT_SCALE][0:1]
    for h in range(halves):
        for x0, size in chunks(L, 32):
            area = pl.ds(x0, size)
            v = vslots[1, h, pl.ds(EDGE + x0, size), :]
            for f, field in enumerate((hwide[h, 0, area, :], v, hwide[h, 1, area, :])):
                left_even[pl.ds(f * L + x0, size), :] = pieces_of(field, v * field)
        right_even[...] = jnp.dot(left_even[...], weights[...], preferred_element_type=F32)
        for x0, size in chunks(L, 32):
            v = vslots[0, h, pl.ds(EDGE + x0, size), :]
            for f in range(3):
                both = right_even[pl.ds(f * L + x0, size), :]
                edges[h, f, pl.ds(x0, size), :] = (v * both[:, :L] + both[:, L:]) * scale8

    stencil = jnp.zeros((L, L), F32)
    for k in range(7):
        stencil = jnp.where(source - target == k - 3, rows[k][0:1], stencil)
    store_weights(weights, stencil)

    source3 = lax.broadcasted_iota(jnp.int32, (2 * L, 2 * L), 0)
    target3 = lanes((2 * L, 2 * L))
    ones = (source3 // L == target3 // L).astype(F32).astype(BF16)
    both = jnp.concatenate([parts[0], parts[1]], axis=1)
    plane_of = lax.rem(lanes((WIDE, 2 * L)), 32)
    group_planes = 4

    def normal_planes(n, carry):
        z0 = group_planes * n
        chosen = [jnp.where(plane_of == z0 + k, both, 0.0).astype(BF16) for k in range(group_planes)]
        found = jnp.dot(jnp.concatenate(chosen, axis=0), ones, preferred_element_type=F32)
        for k in range(group_planes):
            here = found[k * WIDE:k * WIDE + SPAN]
            vel[z0 + k] = frac * here[:, L:] - (crow[z0 + k] + here[:, :L])
        return carry

    lax.fori_loop(0, depth // group_planes, normal_planes, 0)

    def at(z, x0, d):
        return vel[z, pl.ds(EDGE + x0 + d, STEP), :]

    def q_at(f, z, x0, d):
        return uw[f, z, pl.ds(HALO + x0 + d, STEP), :]

    def split(z, left):
        for x0 in range(0, L, STEP):
            v = at(z, x0, 0)
            for f, field in enumerate((q_at(0, z, x0, 0), v, q_at(1, z, x0, 0))):
                left[pl.ds(f * L + x0, STEP), :] = pieces_of(field, v * field)

    def plane(z, left, right, later):
        turn = lax.rem(2 * L - 4 - SLOT * lax.rem(z, half), L)
        right[...] = jnp.dot(left[...], weights[...], preferred_element_type=F32)
        if later is not None:
            split(*later)
        for x0 in range(0, L, STEP):
            own = pl.ds(x0, STEP)
            (along_x,) = skew(lambda d: q_at(0, z, x0, d), (lambda d: at(z, x0, d),))
            (along_z,) = skew(lambda d: q_at(1, around(z, d), x0, 0), (lambda d: at(around(z, d), x0, 0),))
            result[z, 1, own, :] = m120[own, :] * along_x + along_z * (1.0 / 120.0)
        for x0 in range(0, L, STEP):
            own = pl.ds(x0, STEP)
            lane = lanes((STEP, L))
            v = at(z, x0, 0)
            for f in range(3):
                others = result[z, 1, own, :] if f == 1 else part[f // 2, z, own, :]
                turned = pltpu.roll(edges[z // half, f, own, :], turn, 1)
                edge = jnp.where((lane < 4) | (lane >= L - 4), turned, 0.0)
                both = right[pl.ds(f * L + x0, STEP), :]
                result[z, f, own, :] = others + (v * both[:, :L] + both[:, L:]) * scale + edge
        pltpu.make_async_copy(result.at[z], out.at[:, z], out_sem.at[z]).start()

    split(0, left_even)

    def two_planes(n, carry):
        z = 2 * n
        plane(z, left_even, right_even, (z + 1, left_odd))
        plane(z + 1, left_odd, right_odd, (around(z, 2), left_even))
        return carry

    lax.fori_loop(0, depth // 2, two_planes, 0)

    def finish(z, carry):
        pltpu.make_async_copy(result.at[z], out.at[:, z], out_sem.at[z]).wait()
        return carry

    lax.fori_loop(0, depth, finish, 0)


STEP = 32
VMEM_FIRST = 24 * 2**20
VMEM_SECOND = 24 * 2**20


def shards(n_gy, velocity, stream_metric, wall_metric):
    depth = velocity.shape[1]
    halves = depth // min(HALF, depth)
    n_ring = len(rings_of(n_gy))
    others = max(size for _, size in rings_of(n_gy)) - 1
    kept = [
        (2, depth, WIDE, L),
        (depth, SPAN, L),
        (2, 2, L, L),
        (halves, SPAN, L),
        (2, SPAN, L),
        (2, depth, L, L),
        (3, PACKED, L),
        (ROWS, 8, L),
        (L, L),
    ]
    here = pl.BlockSpec(memory_space=pltpu.VMEM)
    anywhere = pl.BlockSpec(memory_space=pl.ANY)
    dma = pltpu.SemaphoreType.DMA
    held = pl.pallas_call(
        functools.partial(first_kernel, n_gy, depth),
        out_shape=[pltpu.VMEM(shape, F32) for shape in kept],
        in_specs=[pl.BlockSpec(memory_space=pltpu.HBM)] * 3,
        out_specs=[here] * len(kept),
        scratch_shapes=[
            pltpu.VMEM((depth, SPAN, L), F32),
            pltpu.VMEM((WIDE, L), F32),
            pltpu.VMEM((3 * L, 2 * L), BF16),
            pltpu.VMEM((3 * halves * L, 2 * L), BF16),
            pltpu.VMEM((2, 2, L, L), F32),
            pltpu.VMEM((2, SPAN, L), F32),
            pltpu.VMEM((n_ring, PACKED, L), F32),
            pltpu.VMEM((n_ring, others, PACKED, L), F32),
            pltpu.VMEM((2, L), F32),
            pltpu.VMEM((n_gy, L), F32),
            pltpu.VMEM((WIDE, 3 * L), BF16),
            pltpu.VMEM((WIDE, 3 * L), BF16),
            dma((4,)), dma((2, 2)), dma((2, 2)), dma((2, 2)), dma((2, 2)),
            dma((n_ring, others)), dma((n_ring, others)),
        ],
        compiler_params=pltpu.CompilerParams(
            collective_id=0, has_side_effects=True, vmem_limit_bytes=VMEM_FIRST),
        name="exchange",
    )(*(pltpu.with_memory_space_constraint(x, pltpu.HBM)
        for x in (velocity, stream_metric.reshape(2, L), wall_metric.reshape(n_gy, L))))
    return pl.pallas_call(
        functools.partial(second_kernel, depth),
        out_shape=jax.ShapeDtypeStruct((3, depth, L, L), F32),
        in_specs=[here] * len(kept),
        out_specs=anywhere,
        scratch_shapes=[
            pltpu.VMEM((depth, SPAN, L), F32),
            pltpu.VMEM((depth, 3, L, L), F32),
            pltpu.VMEM((3, WIDE, L), F32),
            pltpu.VMEM((2, halves, SPAN, L), F32),
            pltpu.VMEM((halves, 3, L, L), F32),
            pltpu.VMEM((6 * L, 2 * L), BF16),
            pltpu.VMEM((6 * L, halves * L), BF16),
            pltpu.VMEM((halves, 2, L, L), F32),
            pltpu.VMEM((3 * L, 6 * L), BF16),
            pltpu.VMEM((3 * L, 6 * L), BF16),
            pltpu.VMEM((3 * L, 2 * L), F32),
            pltpu.VMEM((3 * L, 2 * L), F32),
            dma((depth,)),
        ],
        compiler_params=pltpu.CompilerParams(vmem_limit_bytes=VMEM_SECOND),
        name="advect",
    )(*held)


def solution(mesh):
    spec = P(None, None, "gx", "gy")
    return jax.shard_map(
        functools.partial(shards, mesh.shape["gy"]), mesh=mesh,
        in_specs=(spec, P(), P()), out_specs=spec, check_vma=False)
```

```python
import functools

import jax
import jax.numpy as jnp
from jax import lax
from jax.experimental import pallas as pl
from jax.experimental.pallas import tpu as pltpu
from jax.sharding import PartitionSpec as P

MESH = pl.DeviceIdType.MESH
F32, BF16 = jnp.float32, jnp.bfloat16
L = 128
HALO = 8
EDGE = 4
WIDE = L + 2 * HALO
SPAN = L + 2 * EDGE
CENTRAL = (45.0, -9.0, 1.0)
INTERIOR = (-1.0, 9.0, -45.0, 0.0, 45.0, -9.0, 1.0)
ROW_FIRST = (0.0, 0.0, 0.0, -110.0, 180.0, -90.0, 20.0)
ROW_SECOND = (0.0, 0.0, -20.0, -30.0, 60.0, -10.0, 0.0)
ROW_THIRD = (0.0, 5.0, -40.0, 0.0, 40.0, -5.0, 0.0)
ROW_SECOND_LAST = (0.0, 10.0, -60.0, 30.0, 20.0, 0.0, 0.0)
ROW_LAST = (-20.0, 90.0, -180.0, 110.0, 0.0, 0.0, 0.0)
TILES = SPAN // 8
GROUPS = -(-TILES // 4)
PACKED = 8 * GROUPS
SLOT, HALF = 8, 16
ROW_FRAC, ROW_SCALE, ROW_OWN, ROW_AWAY, ROW_SLOT, ROW_SLOT_SCALE, ROWS = 7, 8, 9, 10, 11, 18, 19


def rings_of(count):
    size = 4 if count % 4 == 0 and count > 16 else 2
    rings, stride = [], 1
    while stride < count:
        rings.append((stride, size))
        stride *= size
    return rings


def lanes(shape):
    return lax.broadcasted_iota(jnp.int32, shape, len(shape) - 1)


def rolled(x, shift):
    if isinstance(shift, int):
        shift %= L
        if shift == 0:
            return x
    return pltpu.roll(x, shift, len(x.shape) - 1)


def running(x):
    lane = lanes(x.shape)
    step = 1
    while step < L:
        x = x + jnp.where(lane >= step, rolled(x, step), 0.0)
        step *= 2
    return x


def scaled(x, weight):
    return x if weight == 1.0 else x * weight


def chunks(total, size):
    return [(min(i, total - size), size) for i in range(0, total, size)]


def three(x):
    high = x.astype(BF16)
    rest = x - high.astype(F32)
    middle = rest.astype(BF16)
    low = (rest - middle.astype(F32)).astype(BF16)
    return high, middle, low


def pieces(x):
    return jnp.concatenate(three(x), axis=1)


def pieces_of(*arrays):
    return jnp.concatenate([part for same in zip(*map(three, arrays)) for part in same], axis=1)


def skew(adv, fields):
    centre = adv(0)
    sums = [None] * len(fields)
    if len(fields) == 1:
        total = None
        for d, weight in enumerate(CENTRAL, start=1):
            term = (centre + adv(d)) * fields[0](d) - (centre + adv(-d)) * fields[0](-d)
            total = scaled(term, weight) if total is None else total + scaled(term, weight)
        return [total]
    for d, weight in enumerate(CENTRAL, start=1):
        up = scaled(centre + adv(d), weight)
        down = scaled(centre + adv(-d), weight)
        for n, field in enumerate(fields):
            term = up * field(d) - down * field(-d)
            sums[n] = term if sums[n] is None else sums[n] + term
    return sums


def slope_sum(field):
    total = None
    for d, weight in enumerate(CENTRAL, start=1):
        term = scaled(field(d) - field(-d), weight)
        total = term if total is None else total + term
    return total


def store_weights(ref, matrix):
    matrix = matrix.astype(BF16)
    nothing = jnp.zeros((L, L), BF16)
    for n in range(3):
        ref[2 * n * L:(2 * n + 1) * L, :] = jnp.concatenate([matrix, nothing], axis=1)
        ref[(2 * n + 1) * L:(2 * n + 2) * L, :] = jnp.concatenate([nothing, matrix], axis=1)


def first_kernel(
    n_gy, depth,
    vel, sm_far, wm_far,
    uw, crow, halo, shalo, sland, part, lines, rows, m120,
    slope, m_wide, ladder, narrowing, hpack, spack, stage_out, stage_in, sm, wm, left_even, left_odd,
    load_sem, gx_send, gx_recv, y_send, y_recv, st_send, st_recv,
):
    gx, gy = lax.axis_index("gx"), lax.axis_index("gy")
    other = 1 - gx
    rings = rings_of(n_gy)
    up_gy, down_gy = lax.rem(gy + 1, n_gy), lax.rem(gy + n_gy - 1, n_gy)
    half = min(HALF, depth)
    halves = depth // half

    def peer(stride, size, offset):
        place = lax.rem(gy // stride, size)
        return gy + (lax.rem(place + offset, size) - place) * stride

    small = [pltpu.make_async_copy(sm_far, sm, load_sem.at[2]), pltpu.make_async_copy(wm_far, wm, load_sem.at[3])]
    for copy in small:
        copy.start()
    loads = []
    for f in range(2):
        loads.append(pltpu.make_async_copy(vel.at[f], uw.at[f, :, pl.ds(HALO, L)], load_sem.at[f]))
        loads[-1].start()

    barrier = pltpu.get_barrier_semaphore()
    count = 0
    targets = [{"gx": other}, {"gy": up_gy}, {"gy": down_gy}]
    for stride, size in rings:
        targets += [{"gy": peer(stride, size, o)} for o in range(1, size)]
    for target in targets:
        pl.semaphore_signal(barrier, inc=1, device_id=target, device_id_type=MESH)
        count += 1

    for copy in small:
        copy.wait()
    rid = lax.broadcasted_iota(jnp.int32, (n_gy, L), 0)
    wall = wm[...]
    recip = 1.0 / wall

    def row_at(values, index):
        picked = jnp.sum(jnp.where(rid == index, values, 0.0), axis=0, keepdims=True)
        return jnp.broadcast_to(picked, (8, L))

    def whole(values):
        return jnp.sum(jnp.sum(values, axis=0, keepdims=True), axis=1, keepdims=True)

    total_h = whole(recip)
    below_h = whole(jnp.where(rid < gy, recip, 0.0))
    r_own, r_next, r_prev = row_at(recip, gy), row_at(recip, up_gy), row_at(recip, down_gy)
    wall_own = row_at(wall, gy)
    lane8 = lanes((8, L))
    run_own, run_next, run_prev = running(r_own), running(r_next), running(r_prev)
    sum_own = jnp.sum(r_own[0:1], axis=1, keepdims=True)
    sum_prev = jnp.sum(r_prev[0:1], axis=1, keepdims=True)
    frac = (below_h + (run_own - 0.5 * r_own)) / total_h
    frac_next = (below_h + sum_own + (run_next - 0.5 * r_next)) / total_h
    frac_prev = (below_h - sum_prev + (run_prev - 0.5 * r_prev)) / total_h
    scale = wall_own * (1.0 / 120.0)
    rows[ROW_FRAC] = frac
    rows[ROW_SCALE] = scale

    def slots(last, first):
        values = jnp.where(lane8 < 4, rolled(last, 4), 0.0)
        values = values + jnp.where((lane8 >= 4) & (lane8 < 8), rolled(first, 4), 0.0)
        step = SLOT
        while step < L:
            values = values + rolled(values, step)
            step *= 2
        return values

    rows[ROW_OWN] = slots(frac, frac)
    rows[ROW_AWAY] = slots(frac_prev, frac_next)
    place = gy * L + lane8
    last_row = n_gy * L - 1
    for k in range(7):
        entry = jnp.full((8, L), INTERIOR[k], F32)
        for row, table in ((0, ROW_FIRST), (1, ROW_SECOND), (2, ROW_THIRD), (last_row - 2, ROW_THIRD),
                           (last_row - 1, ROW_SECOND_LAST), (last_row, ROW_LAST)):
            entry = jnp.where(place == row, table[k], entry)
        rows[k] = entry
        rows[ROW_SLOT + k] = slots(entry, entry)
    rows[ROW_SLOT_SCALE] = slots(scale, scale)
    r60 = r_own[0:1] * (1.0 / 60.0)

    first_row, second_row = sm[0:1, :], sm[1:2, :]
    own_m = jnp.where(gx == 0, first_row, second_row)
    other_m = jnp.where(gx == 0, second_row, first_row)
    own_cols = jnp.broadcast_to(own_m, (L, L)).T
    other_cols = jnp.broadcast_to(other_m, (L, L)).T
    m_wide[0:HALO, :] = other_cols[L - HALO:L, :]
    m_wide[HALO:HALO + L, :] = own_cols
    m_wide[HALO + L:WIDE, :] = other_cols[0:HALO, :]
    m120[...] = own_cols * (1.0 / 120.0)
    source = lax.broadcasted_iota(jnp.int32, (L, 2 * L), 0)
    target = lanes((L, 2 * L))
    steps = jnp.where(source < target, 1.0, jnp.where(source == target, 0.5, 0.0)).astype(BF16)
    for n in range(3):
        ladder[n * L:(n + 1) * L, :] = steps


    def around(z, d):
        return lax.rem(z + (depth + d), depth)

    def plane_terms(z, starts):
        for x0 in starts:
            size = 16

            def at(f):
                return lambda d: uw[f, z, pl.ds(HALO + x0 + d, size), :]

            def over(f):
                return lambda d: uw[f, around(z, d), pl.ds(HALO + x0, size), :]

            along_x = skew(at(0), (at(0), at(1)))
            along_z = skew(over(1), (over(0), over(1)))
            m = m120[pl.ds(x0, size), :]
            for f in range(2):
                part[f, z, pl.ds(x0, size), :] = m * along_x[f] + along_z[f] * (1.0 / 120.0)

    def inner_terms(z, carry):
        plane_terms(z, range(0, L, 16))
        return carry

    def send_slots(source, landing, n):
        copies = []
        for side, where in enumerate((down_gy, up_gy)):
            copies.append(pltpu.make_async_remote_copy(
                src_ref=source.at[side], dst_ref=landing.at[side],
                send_sem=y_send.at[n, side], recv_sem=y_recv.at[n, side],
                device_id={"gy": where}, device_id_type=MESH))
            copies[-1].start()
        return copies

    def pack(read, extent):
        slot = lanes((extent, L)) // SLOT
        result = []
        for h in range(halves):
            def body(z, packed):
                return jnp.where(slot == z, pltpu.roll(read(h * half + z), SLOT * z + 4, 1), packed)

            result.append(lax.fori_loop(0, half, body, jnp.zeros((extent, L), F32), unroll=half))
        return result

    def pack_fields():
        for f in range(2):
            both = jnp.dot(pieces_of(*pack(lambda z, f=f: uw[f, z, pl.ds(HALO, L), :], L)), narrowing[...],
                           preferred_element_type=F32)
            for side in range(2):
                hpack[side, f] = both[:, side * L:(side + 1) * L]

    from_row = lax.broadcasted_iota(jnp.int32, (halves * L, 2 * L), 0)
    to_lane = lanes((halves * L, 2 * L))
    lane, place8 = lax.rem(from_row, L), lax.rem(from_row, SLOT)
    plane_lane = 4 * (half * (from_row // L) + lane // SLOT)
    narrow = ((place8 >= 4) & (to_lane == plane_lane + place8 - 4)) | ((place8 < 4) & (to_lane == L + plane_lane + place8))
    narrow = narrow.astype(F32).astype(BF16)
    for n in range(3):
        narrowing[n * halves * L:(n + 1) * halves * L, :] = narrow

    for copy in loads:
        copy.wait()

    pl.semaphore_wait(barrier, count)

    gx_copies = []
    for f in range(2):
        for side, (src, dst) in enumerate(((L - HALO, 0), (0, HALO + L))):
            gx_copies.append(pltpu.make_async_remote_copy(
                src_ref=vel.at[f, :, pl.ds(src, HALO)], dst_ref=uw.at[f, :, pl.ds(dst, HALO)],
                send_sem=gx_send.at[f, side], recv_sem=gx_recv.at[f, side],
                device_id={"gx": other}, device_id_type=MESH))
            gx_copies[-1].start()

    pack_fields()
    y_copies = send_slots(hpack, halo, 0)

    for copy in gx_copies:
        copy.wait()

    lane_small = lanes((8, L))
    shift = HALO - EDGE

    def slope_split(z, left):
        for x0, size in chunks(SPAN, 48):
            du = slope_sum(lambda d: uw[0, z, pl.ds(shift + x0 + d, size), :])
            dw = slope_sum(lambda d: uw[1, around(z, d), pl.ds(shift + x0, size), :])
            value = (m_wide[pl.ds(shift + x0, size), :] * du + dw) * r60
            slope[z, pl.ds(x0, size), :] = value
            left[pl.ds(min(x0, SPAN - size) + (SLOT if x0 + size == SPAN else 0), size), :] = pieces(value)

    def row_in_left(row):
        return row if row < SPAN - 48 else row + SLOT

    def slope_climb(z, left, sums, later):
        climbed = jnp.dot(left[...], ladder[...], preferred_element_type=F32)
        slope_split(*later)
        for tile in range(TILES):
            row = row_in_left(8 * tile)
            crow[z, pl.ds(8 * tile, 8), :] = climbed[row:row + 8, :L]
            group, quarter = tile // 4, tile % 4
            sums[group] = jnp.where(lane_small == 32 * quarter + z, climbed[row:row + 8, L:], sums[group])
        return sums

    slope_split(0, left_even)

    def slope_plane(n, sums):
        z = 2 * n
        sums = slope_climb(z, left_even, list(sums), (z + 1, left_odd))
        return tuple(slope_climb(z + 1, left_odd, sums, (around(z, 2), left_even)))

    sums = lax.fori_loop(0, depth // 2, slope_plane, tuple(jnp.zeros((8, L), F32) for _ in range(GROUPS)))
    own = jnp.concatenate(sums, axis=0)
    lines[2] = own

    def send_stage(stage):
        stride, size = rings[stage]
        copies = []
        for o in range(1, size):
            copies.append(pltpu.make_async_remote_copy(
                src_ref=stage_out.at[stage], dst_ref=stage_in.at[stage, o - 1],
                send_sem=st_send.at[stage, o - 1], recv_sem=st_recv.at[stage, o - 1],
                device_id={"gy": peer(stride, size, o)}, device_id_type=MESH))
            copies[-1].start()
        return copies

    first_cut, second_cut = ((depth * k) // 32 for k in (8, 20))

    def work(stage):
        if stage == 0:
            for h, value in enumerate(pack(lambda z: slope[z], SPAN)):
                shalo[h] = value
            both = jnp.dot(pieces_of(*(shalo[h] for h in range(halves))), narrowing[...], preferred_element_type=F32)
            for side in range(2):
                spack[side] = both[:, side * L:(side + 1) * L]
            y_copies.extend(send_slots(spack, sland, 1))
            lax.fori_loop(0, first_cut, inner_terms, 0)
        if stage == 1 % len(rings):
            lax.fori_loop(first_cut, second_cut, inner_terms, 0)
        if stage == len(rings) - 1:
            lax.fori_loop(second_cut, depth, inner_terms, 0)

    below = jnp.zeros((PACKED, L), F32)
    for stage, (stride, size) in enumerate(rings):
        stage_out[stage] = own
        copies = send_stage(stage)
        work(stage)
        mine = lax.rem(gy // stride, size)
        for copy in copies:
            copy.wait()
        own = stage_out[stage]
        for o in range(1, size):
            sender = lax.rem(mine + size - o, size)
            value = stage_in[stage, o - 1]
            own = own + value
            below = below + jnp.where(sender < mine, value, 0.0)
        if stage < len(rings) - 1:
            lines[0] = below
            below = lines[0]
    lines[0] = below
    lines[1] = own
    for copy in y_copies:
        copy.wait()


def second_kernel(
    depth, uw, crow, halo, shalo, sland, part, lines, rows, m120,
    out, vel, result, parts, vslots, edges, weights, widening, hwide,
    left_even, left_odd, right_even, right_odd, out_sem,
):
    half = min(HALF, depth)
    halves = depth // half
    frac = rows[ROW_FRAC][0:1]
    scale = rows[ROW_SCALE][0:1]

    def around(z, d):
        return lax.rem(z + (depth + d), depth)

    source = lax.broadcasted_iota(jnp.int32, (L, L), 0)
    target = lanes((L, L))

    packed = pieces(lines[...].reshape(3 * PACKED, L))
    from_lane = lax.broadcasted_iota(jnp.int32, (3 * L, L), 0)
    to_lane = lanes((3 * L, L))
    for quarter in range(4):
        pick = (from_lane // L == to_lane // 32) & (lax.rem(from_lane, L) == 32 * quarter + lax.rem(to_lane, 32))
        found = jnp.dot(packed, pick.astype(F32).astype(BF16), preferred_element_type=F32)
        for group in range(GROUPS):
            tile = 4 * group + quarter
            if tile < TILES:
                for n in range(3):
                    at = n * PACKED + 8 * group
                    parts[n, pl.ds(8 * tile, 8), :] = found[at:at + 8]
    for n in range(3):
        parts[n, pl.ds(SPAN, 8), :] = jnp.zeros((8, L), F32)
    source2 = lax.broadcasted_iota(jnp.int32, (L, halves * L), 0)
    target2 = lanes((L, halves * L))
    to_slot = (lax.rem(source2, 32) == half * (target2 // L) + lax.rem(target2, L) // SLOT) & (source2 < 96)
    to_slot = to_slot.astype(F32).astype(BF16)

    same_slot = source // SLOT == target // SLOT
    place, aim = lax.rem(source, SLOT), lax.rem(target, SLOT)
    passed = ((place >= 4) & (place < aim)) | ((place < 4) & (place > aim))
    same_side = same_slot & ((place >= 4) == (aim >= 4))
    local = jnp.where(same_side & passed, 1.0, jnp.where(source == target, 0.5, 0.0)).astype(BF16)
    local = jnp.concatenate([local, local, local], axis=0)
    first_rows = lax.rem(lanes((SPAN, L)), SLOT) >= 4
    from_row = lax.broadcasted_iota(jnp.int32, (2 * L, halves * L), 0)
    to_lane = lanes((2 * L, halves * L))
    place8 = lax.rem(to_lane, SLOT)
    plane_lane = 4 * (half * (to_lane // L) + lax.rem(to_lane, L) // SLOT)
    widen = ((place8 >= 4) & (from_row == plane_lane + place8 - 4)) | ((place8 < 4) & (from_row == L + plane_lane + place8))
    widen = widen.astype(F32).astype(BF16)
    for n in range(3):
        widening[2 * n * L:2 * (n + 1) * L, :] = widen

    def widened(first, last):
        return jnp.dot(pieces_of(first, last), widening[...], preferred_element_type=F32)

    for f in range(2):
        wide = widened(halo[0, f], halo[1, f])
        for h in range(halves):
            hwide[h, f] = wide[:, h * L:(h + 1) * L]
    swide = widened(sland[0], sland[1])
    spread = [jnp.dot(parts[n].astype(BF16), to_slot, preferred_element_type=F32) for n in range(3)]
    for h in range(halves):
        below, total, line = (x[:SPAN, h * L:(h + 1) * L] for x in spread)
        near = jnp.dot(pieces(shalo[h]), local, preferred_element_type=F32)
        away = jnp.dot(pieces(swide[:, h * L:(h + 1) * L]), local, preferred_element_type=F32)
        near = jnp.where(first_rows, near, line - near)
        away = jnp.where(first_rows, line + away, -away)
        vslots[0, h] = rows[ROW_OWN][0:1] * total - (near + below)
        vslots[1, h] = rows[ROW_AWAY][0:1] * total - (away + below)

    across = same_slot & ((place >= 4) != (aim >= 4))
    stencil = jnp.zeros((L, L), F32)
    for k in range(7):
        stencil = jnp.where(across & (source - target == k - 3), rows[ROW_SLOT + k][0:1], stencil)
    store_weights(weights, stencil)
    scale8 = rows[ROW_SLOT_SCALE][0:1]
    for h in range(halves):
        for x0, size in chunks(L, 32):
            area = pl.ds(x0, size)
            v = vslots[1, h, pl.ds(EDGE + x0, size), :]
            for f, field in enumerate((hwide[h, 0, area, :], v, hwide[h, 1, area, :])):
                left_even[pl.ds(f * L + x0, size), :] = pieces_of(field, v * field)
        right_even[...] = jnp.dot(left_even[...], weights[...], preferred_element_type=F32)
        for x0, size in chunks(L, 32):
            v = vslots[0, h, pl.ds(EDGE + x0, size), :]
            for f in range(3):
                both = right_even[pl.ds(f * L + x0, size), :]
                edges[h, f, pl.ds(x0, size), :] = (v * both[:, :L] + both[:, L:]) * scale8

    stencil = jnp.zeros((L, L), F32)
    for k in range(7):
        stencil = jnp.where(source - target == k - 3, rows[k][0:1], stencil)
    store_weights(weights, stencil)

    source3 = lax.broadcasted_iota(jnp.int32, (2 * L, 2 * L), 0)
    target3 = lanes((2 * L, 2 * L))
    ones = (source3 // L == target3 // L).astype(F32).astype(BF16)
    both = jnp.concatenate([parts[0], parts[1]], axis=1)
    plane_of = lax.rem(lanes((WIDE, 2 * L)), 32)
    group_planes = 4

    def normal_planes(n, carry):
        z0 = group_planes * n
        chosen = [jnp.where(plane_of == z0 + k, both, 0.0).astype(BF16) for k in range(group_planes)]
        found = jnp.dot(jnp.concatenate(chosen, axis=0), ones, preferred_element_type=F32)
        for k in range(group_planes):
            here = found[k * WIDE:k * WIDE + SPAN]
            vel[z0 + k] = frac * here[:, L:] - (crow[z0 + k] + here[:, :L])
        return carry

    lax.fori_loop(0, depth // group_planes, normal_planes, 0, unroll=2)

    def at(z, x0, d):
        return vel[z, pl.ds(EDGE + x0 + d, STEP), :]

    def q_at(f, z, x0, d):
        return uw[f, z, pl.ds(HALO + x0 + d, STEP), :]

    def split(z, left):
        for x0 in range(0, L, STEP):
            v = at(z, x0, 0)
            for f, field in enumerate((q_at(0, z, x0, 0), v, q_at(1, z, x0, 0))):
                left[pl.ds(f * L + x0, STEP), :] = pieces_of(field, v * field)

    def plane(z, left, right, later):
        turn = lax.rem(2 * L - 4 - SLOT * lax.rem(z, half), L)
        right[...] = jnp.dot(left[...], weights[...], preferred_element_type=F32)
        if later is not None:
            split(*later)
        for x0 in range(0, L, STEP):
            own = pl.ds(x0, STEP)
            (along_x,) = skew(lambda d: q_at(0, z, x0, d), (lambda d: at(z, x0, d),))
            (along_z,) = skew(lambda d: q_at(1, around(z, d), x0, 0), (lambda d: at(around(z, d), x0, 0),))
            result[z, 1, own, :] = m120[own, :] * along_x + along_z * (1.0 / 120.0)
        for x0 in range(0, L, STEP):
            own = pl.ds(x0, STEP)
            lane = lanes((STEP, L))
            v = at(z, x0, 0)
            for f in range(3):
                others = result[z, 1, own, :] if f == 1 else part[f // 2, z, own, :]
                turned = pltpu.roll(edges[z // half, f, own, :], turn, 1)
                edge = jnp.where((lane < 4) | (lane >= L - 4), turned, 0.0)
                both = right[pl.ds(f * L + x0, STEP), :]
                result[z, f, own, :] = others + (v * both[:, :L] + both[:, L:]) * scale + edge
        pltpu.make_async_copy(result.at[z], out.at[:, z], out_sem.at[z]).start()

    split(0, left_even)

    def two_planes(n, carry):
        z = 2 * n
        plane(z, left_even, right_even, (z + 1, left_odd))
        plane(z + 1, left_odd, right_odd, (around(z, 2), left_even))
        return carry

    lax.fori_loop(0, depth // 2, two_planes, 0)

    def finish(z, carry):
        pltpu.make_async_copy(result.at[z], out.at[:, z], out_sem.at[z]).wait()
        return carry

    lax.fori_loop(0, depth, finish, 0)


STEP = 32
VMEM_FIRST = 24 * 2**20
VMEM_SECOND = 24 * 2**20


def shards(n_gy, velocity, stream_metric, wall_metric):
    depth = velocity.shape[1]
    halves = depth // min(HALF, depth)
    n_ring = len(rings_of(n_gy))
    others = max(size for _, size in rings_of(n_gy)) - 1
    kept = [
        (2, depth, WIDE, L),
        (depth, SPAN, L),
        (2, 2, L, L),
        (halves, SPAN, L),
        (2, SPAN, L),
        (2, depth, L, L),
        (3, PACKED, L),
        (ROWS, 8, L),
        (L, L),
    ]
    here = pl.BlockSpec(memory_space=pltpu.VMEM)
    anywhere = pl.BlockSpec(memory_space=pl.ANY)
    dma = pltpu.SemaphoreType.DMA
    held = pl.pallas_call(
        functools.partial(first_kernel, n_gy, depth),
        out_shape=[pltpu.VMEM(shape, F32) for shape in kept],
        in_specs=[pl.BlockSpec(memory_space=pltpu.HBM)] * 3,
        out_specs=[here] * len(kept),
        scratch_shapes=[
            pltpu.VMEM((depth, SPAN, L), F32),
            pltpu.VMEM((WIDE, L), F32),
            pltpu.VMEM((3 * L, 2 * L), BF16),
            pltpu.VMEM((3 * halves * L, 2 * L), BF16),
            pltpu.VMEM((2, 2, L, L), F32),
            pltpu.VMEM((2, SPAN, L), F32),
            pltpu.VMEM((n_ring, PACKED, L), F32),
            pltpu.VMEM((n_ring, others, PACKED, L), F32),
            pltpu.VMEM((2, L), F32),
            pltpu.VMEM((n_gy, L), F32),
            pltpu.VMEM((WIDE, 3 * L), BF16),
            pltpu.VMEM((WIDE, 3 * L), BF16),
            dma((4,)), dma((2, 2)), dma((2, 2)), dma((2, 2)), dma((2, 2)),
            dma((n_ring, others)), dma((n_ring, others)),
        ],
        compiler_params=pltpu.CompilerParams(
            collective_id=0, has_side_effects=True, vmem_limit_bytes=VMEM_FIRST),
        name="exchange",
    )(*(pltpu.with_memory_space_constraint(x, pltpu.HBM)
        for x in (velocity, stream_metric.reshape(2, L), wall_metric.reshape(n_gy, L))))
    return pl.pallas_call(
        functools.partial(second_kernel, depth),
        out_shape=jax.ShapeDtypeStruct((3, depth, L, L), F32),
        in_specs=[here] * len(kept),
        out_specs=anywhere,
        scratch_shapes=[
            pltpu.VMEM((depth, SPAN, L), F32),
            pltpu.VMEM((depth, 3, L, L), F32),
            pltpu.VMEM((3, WIDE, L), F32),
            pltpu.VMEM((2, halves, SPAN, L), F32),
            pltpu.VMEM((halves, 3, L, L), F32),
            pltpu.VMEM((6 * L, 2 * L), BF16),
            pltpu.VMEM((6 * L, halves * L), BF16),
            pltpu.VMEM((halves, 2, L, L), F32),
            pltpu.VMEM((3 * L, 6 * L), BF16),
            pltpu.VMEM((3 * L, 6 * L), BF16),
            pltpu.VMEM((3 * L, 2 * L), F32),
            pltpu.VMEM((3 * L, 2 * L), F32),
            dma((depth,)),
        ],
        compiler_params=pltpu.CompilerParams(vmem_limit_bytes=VMEM_SECOND),
        name="advect",
    )(*held)


def solution(mesh):
    spec = P(None, None, "gx", "gy")
    return jax.shard_map(
        functools.partial(shards, mesh.shape["gy"]), mesh=mesh,
        in_specs=(spec, P(), P()), out_specs=spec, check_vma=False)
```

```python
import functools

import jax
import jax.numpy as jnp
from jax import lax
from jax.experimental import pallas as pl
from jax.experimental.pallas import tpu as pltpu
from jax.sharding import PartitionSpec as P

MESH = pl.DeviceIdType.MESH
F32, BF16 = jnp.float32, jnp.bfloat16
L = 128
HALO = 8
EDGE = 4
WIDE = L + 2 * HALO
SPAN = L + 2 * EDGE
CENTRAL = (45.0, -9.0, 1.0)
INTERIOR = (-1.0, 9.0, -45.0, 0.0, 45.0, -9.0, 1.0)
ROW_FIRST = (0.0, 0.0, 0.0, -110.0, 180.0, -90.0, 20.0)
ROW_SECOND = (0.0, 0.0, -20.0, -30.0, 60.0, -10.0, 0.0)
ROW_THIRD = (0.0, 5.0, -40.0, 0.0, 40.0, -5.0, 0.0)
ROW_SECOND_LAST = (0.0, 10.0, -60.0, 30.0, 20.0, 0.0, 0.0)
ROW_LAST = (-20.0, 90.0, -180.0, 110.0, 0.0, 0.0, 0.0)
TILES = SPAN // 8
GROUPS = -(-TILES // 4)
PACKED = 8 * GROUPS
SLOT, HALF = 8, 16
ROW_FRAC, ROW_SCALE, ROW_OWN, ROW_AWAY, ROW_SLOT, ROW_SLOT_SCALE, ROWS = 7, 8, 9, 10, 11, 18, 19


def rings_of(count):
    size = 4 if count % 4 == 0 and count > 16 else 2
    rings, stride = [], 1
    while stride < count:
        rings.append((stride, size))
        stride *= size
    return rings


def lanes(shape):
    return lax.broadcasted_iota(jnp.int32, shape, len(shape) - 1)


def rolled(x, shift):
    if isinstance(shift, int):
        shift %= L
        if shift == 0:
            return x
    return pltpu.roll(x, shift, len(x.shape) - 1)


def running(x):
    lane = lanes(x.shape)
    step = 1
    while step < L:
        x = x + jnp.where(lane >= step, rolled(x, step), 0.0)
        step *= 2
    return x


def scaled(x, weight):
    return x if weight == 1.0 else x * weight


def chunks(total, size):
    return [(min(i, total - size), size) for i in range(0, total, size)]


def three(x):
    high = x.astype(BF16)
    rest = x - high.astype(F32)
    middle = rest.astype(BF16)
    low = (rest - middle.astype(F32)).astype(BF16)
    return high, middle, low


def pieces(x):
    return jnp.concatenate(three(x), axis=1)


def pieces_of(*arrays):
    return jnp.concatenate([part for same in zip(*map(three, arrays)) for part in same], axis=1)


def skew(adv, fields):
    centre = adv(0)
    sums = [None] * len(fields)
    if len(fields) == 1:
        total = None
        for d, weight in enumerate(CENTRAL, start=1):
            term = (centre + adv(d)) * fields[0](d) - (centre + adv(-d)) * fields[0](-d)
            total = scaled(term, weight) if total is None else total + scaled(term, weight)
        return [total]
    for d, weight in enumerate(CENTRAL, start=1):
        up = scaled(centre + adv(d), weight)
        down = scaled(centre + adv(-d), weight)
        for n, field in enumerate(fields):
            term = up * field(d) - down * field(-d)
            sums[n] = term if sums[n] is None else sums[n] + term
    return sums


def slope_sum(field):
    total = None
    for d, weight in enumerate(CENTRAL, start=1):
        term = scaled(field(d) - field(-d), weight)
        total = term if total is None else total + term
    return total


def store_weights(ref, matrix):
    matrix = matrix.astype(BF16)
    nothing = jnp.zeros((L, L), BF16)
    for n in range(3):
        ref[2 * n * L:(2 * n + 1) * L, :] = jnp.concatenate([matrix, nothing], axis=1)
        ref[(2 * n + 1) * L:(2 * n + 2) * L, :] = jnp.concatenate([nothing, matrix], axis=1)


def first_kernel(
    n_gy, depth,
    vel, sm_far, wm_far,
    uw, crow, halo, shalo, sland, part, lines, rows, m120,
    slope, m_wide, ladder, narrowing, hpack, spack, stage_out, stage_in, sm, wm, left_even, left_odd,
    load_sem, gx_send, gx_recv, y_send, y_recv, st_send, st_recv,
):
    gx, gy = lax.axis_index("gx"), lax.axis_index("gy")
    other = 1 - gx
    rings = rings_of(n_gy)
    up_gy, down_gy = lax.rem(gy + 1, n_gy), lax.rem(gy + n_gy - 1, n_gy)
    half = min(HALF, depth)
    halves = depth // half

    def peer(stride, size, offset):
        place = lax.rem(gy // stride, size)
        return gy + (lax.rem(place + offset, size) - place) * stride

    small = [pltpu.make_async_copy(sm_far, sm, load_sem.at[2]), pltpu.make_async_copy(wm_far, wm, load_sem.at[3])]
    for copy in small:
        copy.start()
    loads = []
    for f in range(2):
        loads.append(pltpu.make_async_copy(vel.at[f], uw.at[f, :, pl.ds(HALO, L)], load_sem.at[f]))
        loads[-1].start()

    barrier = pltpu.get_barrier_semaphore()
    count = 0
    targets = [{"gx": other}, {"gy": up_gy}, {"gy": down_gy}]
    for stride, size in rings:
        targets += [{"gy": peer(stride, size, o)} for o in range(1, size)]
    for target in targets:
        pl.semaphore_signal(barrier, inc=1, device_id=target, device_id_type=MESH)
        count += 1

    for copy in small:
        copy.wait()
    rid = lax.broadcasted_iota(jnp.int32, (n_gy, L), 0)
    wall = wm[...]
    recip = 1.0 / wall

    def row_at(values, index):
        picked = jnp.sum(jnp.where(rid == index, values, 0.0), axis=0, keepdims=True)
        return jnp.broadcast_to(picked, (8, L))

    def whole(values):
        return jnp.sum(jnp.sum(values, axis=0, keepdims=True), axis=1, keepdims=True)

    total_h = whole(recip)
    below_h = whole(jnp.where(rid < gy, recip, 0.0))
    r_own, r_next, r_prev = row_at(recip, gy), row_at(recip, up_gy), row_at(recip, down_gy)
    wall_own = row_at(wall, gy)
    lane8 = lanes((8, L))
    run_own, run_next, run_prev = running(r_own), running(r_next), running(r_prev)
    sum_own = jnp.sum(r_own[0:1], axis=1, keepdims=True)
    sum_prev = jnp.sum(r_prev[0:1], axis=1, keepdims=True)
    frac = (below_h + (run_own - 0.5 * r_own)) / total_h
    frac_next = (below_h + sum_own + (run_next - 0.5 * r_next)) / total_h
    frac_prev = (below_h - sum_prev + (run_prev - 0.5 * r_prev)) / total_h
    scale = wall_own * (1.0 / 120.0)
    rows[ROW_FRAC] = frac
    rows[ROW_SCALE] = scale

    def slots(last, first):
        values = jnp.where(lane8 < 4, rolled(last, 4), 0.0)
        values = values + jnp.where((lane8 >= 4) & (lane8 < 8), rolled(first, 4), 0.0)
        step = SLOT
        while step < L:
            values = values + rolled(values, step)
            step *= 2
        return values

    rows[ROW_OWN] = slots(frac, frac)
    rows[ROW_AWAY] = slots(frac_prev, frac_next)
    place = gy * L + lane8
    last_row = n_gy * L - 1
    for k in range(7):
        entry = jnp.full((8, L), INTERIOR[k], F32)
        for row, table in ((0, ROW_FIRST), (1, ROW_SECOND), (2, ROW_THIRD), (last_row - 2, ROW_THIRD),
                           (last_row - 1, ROW_SECOND_LAST), (last_row, ROW_LAST)):
            entry = jnp.where(place == row, table[k], entry)
        rows[k] = entry
        rows[ROW_SLOT + k] = slots(entry, entry)
    rows[ROW_SLOT_SCALE] = slots(scale, scale)
    r60 = r_own[0:1] * (1.0 / 60.0)

    first_row, second_row = sm[0:1, :], sm[1:2, :]
    own_m = jnp.where(gx == 0, first_row, second_row)
    other_m = jnp.where(gx == 0, second_row, first_row)
    own_cols = jnp.broadcast_to(own_m, (L, L)).T
    other_cols = jnp.broadcast_to(other_m, (L, L)).T
    m_wide[0:HALO, :] = other_cols[L - HALO:L, :]
    m_wide[HALO:HALO + L, :] = own_cols
    m_wide[HALO + L:WIDE, :] = other_cols[0:HALO, :]
    m120[...] = own_cols * (1.0 / 120.0)
    source = lax.broadcasted_iota(jnp.int32, (L, 2 * L), 0)
    target = lanes((L, 2 * L))
    steps = jnp.where(source < target, 1.0, jnp.where(source == target, 0.5, 0.0)).astype(BF16)
    for n in range(3):
        ladder[n * L:(n + 1) * L, :] = steps


    def around(z, d):
        return lax.rem(z + (depth + d), depth)

    def plane_terms(z, starts):
        for x0 in starts:
            size = 16

            def at(f):
                return lambda d: uw[f, z, pl.ds(HALO + x0 + d, size), :]

            def over(f):
                return lambda d: uw[f, around(z, d), pl.ds(HALO + x0, size), :]

            along_x = skew(at(0), (at(0), at(1)))
            along_z = skew(over(1), (over(0), over(1)))
            m = m120[pl.ds(x0, size), :]
            for f in range(2):
                part[f, z, pl.ds(x0, size), :] = m * along_x[f] + along_z[f] * (1.0 / 120.0)

    def inner_terms(z, carry):
        plane_terms(z, range(0, L, 16))
        return carry

    def send_slots(source, landing, n):
        copies = []
        for side, where in enumerate((down_gy, up_gy)):
            copies.append(pltpu.make_async_remote_copy(
                src_ref=source.at[side], dst_ref=landing.at[side],
                send_sem=y_send.at[n, side], recv_sem=y_recv.at[n, side],
                device_id={"gy": where}, device_id_type=MESH))
            copies[-1].start()
        return copies

    def pack(read, extent):
        slot = lanes((extent, L)) // SLOT
        result = []
        for h in range(halves):
            def body(z, packed):
                return jnp.where(slot == z, pltpu.roll(read(h * half + z), SLOT * z + 4, 1), packed)

            result.append(lax.fori_loop(0, half, body, jnp.zeros((extent, L), F32), unroll=half))
        return result

    def pack_fields():
        for f in range(2):
            both = jnp.dot(pieces_of(*pack(lambda z, f=f: uw[f, z, pl.ds(HALO, L), :], L)), narrowing[...],
                           preferred_element_type=F32)
            for side in range(2):
                hpack[side, f] = both[:, side * L:(side + 1) * L]

    from_row = lax.broadcasted_iota(jnp.int32, (halves * L, 2 * L), 0)
    to_lane = lanes((halves * L, 2 * L))
    lane, place8 = lax.rem(from_row, L), lax.rem(from_row, SLOT)
    plane_lane = 4 * (half * (from_row // L) + lane // SLOT)
    narrow = ((place8 >= 4) & (to_lane == plane_lane + place8 - 4)) | ((place8 < 4) & (to_lane == L + plane_lane + place8))
    narrow = narrow.astype(F32).astype(BF16)
    for n in range(3):
        narrowing[n * halves * L:(n + 1) * halves * L, :] = narrow

    for copy in loads:
        copy.wait()

    pl.semaphore_wait(barrier, count)

    gx_copies = []
    for f in range(2):
        for side, (src, dst) in enumerate(((L - HALO, 0), (0, HALO + L))):
            gx_copies.append(pltpu.make_async_remote_copy(
                src_ref=vel.at[f, :, pl.ds(src, HALO)], dst_ref=uw.at[f, :, pl.ds(dst, HALO)],
                send_sem=gx_send.at[f, side], recv_sem=gx_recv.at[f, side],
                device_id={"gx": other}, device_id_type=MESH))
            gx_copies[-1].start()

    pack_fields()
    y_copies = send_slots(hpack, halo, 0)

    for copy in gx_copies:
        copy.wait()

    lane_small = lanes((8, L))
    shift = HALO - EDGE

    def slope_split(z, left):
        for x0, size in chunks(SPAN, 48):
            du = slope_sum(lambda d: uw[0, z, pl.ds(shift + x0 + d, size), :])
            dw = slope_sum(lambda d: uw[1, around(z, d), pl.ds(shift + x0, size), :])
            value = (m_wide[pl.ds(shift + x0, size), :] * du + dw) * r60
            slope[z, pl.ds(x0, size), :] = value
            left[pl.ds(min(x0, SPAN - size) + (SLOT if x0 + size == SPAN else 0), size), :] = pieces(value)

    def row_in_left(row):
        return row if row < SPAN - 48 else row + SLOT

    def slope_climb(z, left, sums, later):
        climbed = jnp.dot(left[...], ladder[...], preferred_element_type=F32)
        slope_split(*later)
        for tile in range(TILES):
            row = row_in_left(8 * tile)
            crow[z, pl.ds(8 * tile, 8), :] = climbed[row:row + 8, :L]
            group, quarter = tile // 4, tile % 4
            sums[group] = jnp.where(lane_small == 32 * quarter + z, climbed[row:row + 8, L:], sums[group])
        return sums

    slope_split(0, left_even)

    def slope_plane(n, sums):
        z = 2 * n
        sums = slope_climb(z, left_even, list(sums), (z + 1, left_odd))
        return tuple(slope_climb(z + 1, left_odd, sums, (around(z, 2), left_even)))

    sums = lax.fori_loop(0, depth // 2, slope_plane, tuple(jnp.zeros((8, L), F32) for _ in range(GROUPS)), unroll=2)
    own = jnp.concatenate(sums, axis=0)
    lines[2] = own

    def send_stage(stage):
        stride, size = rings[stage]
        copies = []
        for o in range(1, size):
            copies.append(pltpu.make_async_remote_copy(
                src_ref=stage_out.at[stage], dst_ref=stage_in.at[stage, o - 1],
                send_sem=st_send.at[stage, o - 1], recv_sem=st_recv.at[stage, o - 1],
                device_id={"gy": peer(stride, size, o)}, device_id_type=MESH))
            copies[-1].start()
        return copies

    first_cut, second_cut = ((depth * k) // 32 for k in (8, 20))

    def work(stage):
        if stage == 0:
            for h, value in enumerate(pack(lambda z: slope[z], SPAN)):
                shalo[h] = value
            both = jnp.dot(pieces_of(*(shalo[h] for h in range(halves))), narrowing[...], preferred_element_type=F32)
            for side in range(2):
                spack[side] = both[:, side * L:(side + 1) * L]
            y_copies.extend(send_slots(spack, sland, 1))
            lax.fori_loop(0, first_cut, inner_terms, 0)
        if stage == 1 % len(rings):
            lax.fori_loop(first_cut, second_cut, inner_terms, 0)
        if stage == len(rings) - 1:
            lax.fori_loop(second_cut, depth, inner_terms, 0)

    below = jnp.zeros((PACKED, L), F32)
    for stage, (stride, size) in enumerate(rings):
        stage_out[stage] = own
        copies = send_stage(stage)
        work(stage)
        mine = lax.rem(gy // stride, size)
        for copy in copies:
            copy.wait()
        own = stage_out[stage]
        for o in range(1, size):
            sender = lax.rem(mine + size - o, size)
            value = stage_in[stage, o - 1]
            own = own + value
            below = below + jnp.where(sender < mine, value, 0.0)
        if stage < len(rings) - 1:
            lines[0] = below
            below = lines[0]
    lines[0] = below
    lines[1] = own
    for copy in y_copies:
        copy.wait()


def second_kernel(
    depth, uw, crow, halo, shalo, sland, part, lines, rows, m120,
    out, vel, result, parts, vslots, edges, weights, widening, hwide,
    left_even, left_odd, right_even, right_odd, out_sem,
):
    half = min(HALF, depth)
    halves = depth // half
    frac = rows[ROW_FRAC][0:1]
    scale = rows[ROW_SCALE][0:1]

    def around(z, d):
        return lax.rem(z + (depth + d), depth)

    source = lax.broadcasted_iota(jnp.int32, (L, L), 0)
    target = lanes((L, L))

    packed = pieces(lines[...].reshape(3 * PACKED, L))
    from_lane = lax.broadcasted_iota(jnp.int32, (3 * L, L), 0)
    to_lane = lanes((3 * L, L))
    for quarter in range(4):
        pick = (from_lane // L == to_lane // 32) & (lax.rem(from_lane, L) == 32 * quarter + lax.rem(to_lane, 32))
        found = jnp.dot(packed, pick.astype(F32).astype(BF16), preferred_element_type=F32)
        for group in range(GROUPS):
            tile = 4 * group + quarter
            if tile < TILES:
                for n in range(3):
                    at = n * PACKED + 8 * group
                    parts[n, pl.ds(8 * tile, 8), :] = found[at:at + 8]
    for n in range(3):
        parts[n, pl.ds(SPAN, 8), :] = jnp.zeros((8, L), F32)
    source2 = lax.broadcasted_iota(jnp.int32, (L, halves * L), 0)
    target2 = lanes((L, halves * L))
    to_slot = (lax.rem(source2, 32) == half * (target2 // L) + lax.rem(target2, L) // SLOT) & (source2 < 96)
    to_slot = to_slot.astype(F32).astype(BF16)

    same_slot = source // SLOT == target // SLOT
    place, aim = lax.rem(source, SLOT), lax.rem(target, SLOT)
    passed = ((place >= 4) & (place < aim)) | ((place < 4) & (place > aim))
    same_side = same_slot & ((place >= 4) == (aim >= 4))
    local = jnp.where(same_side & passed, 1.0, jnp.where(source == target, 0.5, 0.0)).astype(BF16)
    local = jnp.concatenate([local, local, local], axis=0)
    first_rows = lax.rem(lanes((SPAN, L)), SLOT) >= 4
    from_row = lax.broadcasted_iota(jnp.int32, (2 * L, halves * L), 0)
    to_lane = lanes((2 * L, halves * L))
    place8 = lax.rem(to_lane, SLOT)
    plane_lane = 4 * (half * (to_lane // L) + lax.rem(to_lane, L) // SLOT)
    widen = ((place8 >= 4) & (from_row == plane_lane + place8 - 4)) | ((place8 < 4) & (from_row == L + plane_lane + place8))
    widen = widen.astype(F32).astype(BF16)
    for n in range(3):
        widening[2 * n * L:2 * (n + 1) * L, :] = widen

    def widened(first, last):
        return jnp.dot(pieces_of(first, last), widening[...], preferred_element_type=F32)

    for f in range(2):
        wide = widened(halo[0, f], halo[1, f])
        for h in range(halves):
            hwide[h, f] = wide[:, h * L:(h + 1) * L]
    swide = widened(sland[0], sland[1])
    spread = [jnp.dot(parts[n].astype(BF16), to_slot, preferred_element_type=F32) for n in range(3)]
    for h in range(halves):
        below, total, line = (x[:SPAN, h * L:(h + 1) * L] for x in spread)
        near = jnp.dot(pieces(shalo[h]), local, preferred_element_type=F32)
        away = jnp.dot(pieces(swide[:, h * L:(h + 1) * L]), local, preferred_element_type=F32)
        near = jnp.where(first_rows, near, line - near)
        away = jnp.where(first_rows, line + away, -away)
        vslots[0, h] = rows[ROW_OWN][0:1] * total - (near + below)
        vslots[1, h] = rows[ROW_AWAY][0:1] * total - (away + below)

    across = same_slot & ((place >= 4) != (aim >= 4))
    stencil = jnp.zeros((L, L), F32)
    for k in range(7):
        stencil = jnp.where(across & (source - target == k - 3), rows[ROW_SLOT + k][0:1], stencil)
    store_weights(weights, stencil)
    scale8 = rows[ROW_SLOT_SCALE][0:1]
    for h in range(halves):
        for x0, size in chunks(L, 32):
            area = pl.ds(x0, size)
            v = vslots[1, h, pl.ds(EDGE + x0, size), :]
            for f, field in enumerate((hwide[h, 0, area, :], v, hwide[h, 1, area, :])):
                left_even[pl.ds(f * L + x0, size), :] = pieces_of(field, v * field)
        right_even[...] = jnp.dot(left_even[...], weights[...], preferred_element_type=F32)
        for x0, size in chunks(L, 32):
            v = vslots[0, h, pl.ds(EDGE + x0, size), :]
            for f in range(3):
                both = right_even[pl.ds(f * L + x0, size), :]
                edges[h, f, pl.ds(x0, size), :] = (v * both[:, :L] + both[:, L:]) * scale8

    stencil = jnp.zeros((L, L), F32)
    for k in range(7):
        stencil = jnp.where(source - target == k - 3, rows[k][0:1], stencil)
    store_weights(weights, stencil)

    source3 = lax.broadcasted_iota(jnp.int32, (2 * L, 2 * L), 0)
    target3 = lanes((2 * L, 2 * L))
    ones = (source3 // L == target3 // L).astype(F32).astype(BF16)
    both = jnp.concatenate([parts[0], parts[1]], axis=1)
    plane_of = lax.rem(lanes((WIDE, 2 * L)), 32)
    group_planes = 4

    def normal_planes(n, carry):
        z0 = group_planes * n
        chosen = [jnp.where(plane_of == z0 + k, both, 0.0).astype(BF16) for k in range(group_planes)]
        found = jnp.dot(jnp.concatenate(chosen, axis=0), ones, preferred_element_type=F32)
        for k in range(group_planes):
            here = found[k * WIDE:k * WIDE + SPAN]
            vel[z0 + k] = frac * here[:, L:] - (crow[z0 + k] + here[:, :L])
        return carry

    lax.fori_loop(0, depth // group_planes, normal_planes, 0, unroll=2)

    def at(z, x0, d):
        return vel[z, pl.ds(EDGE + x0 + d, STEP), :]

    def q_at(f, z, x0, d):
        return uw[f, z, pl.ds(HALO + x0 + d, STEP), :]

    def split(z, left):
        for x0 in range(0, L, STEP):
            v = at(z, x0, 0)
            for f, field in enumerate((q_at(0, z, x0, 0), v, q_at(1, z, x0, 0))):
                left[pl.ds(f * L + x0, STEP), :] = pieces_of(field, v * field)

    def plane(z, left, right, later):
        turn = lax.rem(2 * L - 4 - SLOT * lax.rem(z, half), L)
        right[...] = jnp.dot(left[...], weights[...], preferred_element_type=F32)
        if later is not None:
            split(*later)
        for x0 in range(0, L, STEP):
            own = pl.ds(x0, STEP)
            (along_x,) = skew(lambda d: q_at(0, z, x0, d), (lambda d: at(z, x0, d),))
            (along_z,) = skew(lambda d: q_at(1, around(z, d), x0, 0), (lambda d: at(around(z, d), x0, 0),))
            result[z, 1, own, :] = m120[own, :] * along_x + along_z * (1.0 / 120.0)
        for x0 in range(0, L, STEP):
            own = pl.ds(x0, STEP)
            lane = lanes((STEP, L))
            v = at(z, x0, 0)
            for f in range(3):
                others = result[z, 1, own, :] if f == 1 else part[f // 2, z, own, :]
                turned = pltpu.roll(edges[z // half, f, own, :], turn, 1)
                edge = jnp.where((lane < 4) | (lane >= L - 4), turned, 0.0)
                both = right[pl.ds(f * L + x0, STEP), :]
                result[z, f, own, :] = others + (v * both[:, :L] + both[:, L:]) * scale + edge
        pltpu.make_async_copy(result.at[z], out.at[:, z], out_sem.at[z]).start()

    split(0, left_even)

    def two_planes(n, carry):
        z = 2 * n
        plane(z, left_even, right_even, (z + 1, left_odd))
        plane(z + 1, left_odd, right_odd, (around(z, 2), left_even))
        return carry

    lax.fori_loop(0, depth // 2, two_planes, 0)

    def finish(z, carry):
        pltpu.make_async_copy(result.at[z], out.at[:, z], out_sem.at[z]).wait()
        return carry

    lax.fori_loop(0, depth, finish, 0)


STEP = 32
VMEM_FIRST = 24 * 2**20
VMEM_SECOND = 24 * 2**20


def shards(n_gy, velocity, stream_metric, wall_metric):
    depth = velocity.shape[1]
    halves = depth // min(HALF, depth)
    n_ring = len(rings_of(n_gy))
    others = max(size for _, size in rings_of(n_gy)) - 1
    kept = [
        (2, depth, WIDE, L),
        (depth, SPAN, L),
        (2, 2, L, L),
        (halves, SPAN, L),
        (2, SPAN, L),
        (2, depth, L, L),
        (3, PACKED, L),
        (ROWS, 8, L),
        (L, L),
    ]
    here = pl.BlockSpec(memory_space=pltpu.VMEM)
    anywhere = pl.BlockSpec(memory_space=pl.ANY)
    dma = pltpu.SemaphoreType.DMA
    held = pl.pallas_call(
        functools.partial(first_kernel, n_gy, depth),
        out_shape=[pltpu.VMEM(shape, F32) for shape in kept],
        in_specs=[pl.BlockSpec(memory_space=pltpu.HBM)] * 3,
        out_specs=[here] * len(kept),
        scratch_shapes=[
            pltpu.VMEM((depth, SPAN, L), F32),
            pltpu.VMEM((WIDE, L), F32),
            pltpu.VMEM((3 * L, 2 * L), BF16),
            pltpu.VMEM((3 * halves * L, 2 * L), BF16),
            pltpu.VMEM((2, 2, L, L), F32),
            pltpu.VMEM((2, SPAN, L), F32),
            pltpu.VMEM((n_ring, PACKED, L), F32),
            pltpu.VMEM((n_ring, others, PACKED, L), F32),
            pltpu.VMEM((2, L), F32),
            pltpu.VMEM((n_gy, L), F32),
            pltpu.VMEM((WIDE, 3 * L), BF16),
            pltpu.VMEM((WIDE, 3 * L), BF16),
            dma((4,)), dma((2, 2)), dma((2, 2)), dma((2, 2)), dma((2, 2)),
            dma((n_ring, others)), dma((n_ring, others)),
        ],
        compiler_params=pltpu.CompilerParams(
            collective_id=0, has_side_effects=True, vmem_limit_bytes=VMEM_FIRST),
        name="exchange",
    )(*(pltpu.with_memory_space_constraint(x, pltpu.HBM)
        for x in (velocity, stream_metric.reshape(2, L), wall_metric.reshape(n_gy, L))))
    return pl.pallas_call(
        functools.partial(second_kernel, depth),
        out_shape=jax.ShapeDtypeStruct((3, depth, L, L), F32),
        in_specs=[here] * len(kept),
        out_specs=anywhere,
        scratch_shapes=[
            pltpu.VMEM((depth, SPAN, L), F32),
            pltpu.VMEM((depth, 3, L, L), F32),
            pltpu.VMEM((3, WIDE, L), F32),
            pltpu.VMEM((2, halves, SPAN, L), F32),
            pltpu.VMEM((halves, 3, L, L), F32),
            pltpu.VMEM((6 * L, 2 * L), BF16),
            pltpu.VMEM((6 * L, halves * L), BF16),
            pltpu.VMEM((halves, 2, L, L), F32),
            pltpu.VMEM((3 * L, 6 * L), BF16),
            pltpu.VMEM((3 * L, 6 * L), BF16),
            pltpu.VMEM((3 * L, 2 * L), F32),
            pltpu.VMEM((3 * L, 2 * L), F32),
            dma((depth,)),
        ],
        compiler_params=pltpu.CompilerParams(vmem_limit_bytes=VMEM_SECOND),
        name="advect",
    )(*held)


def solution(mesh):
    spec = P(None, None, "gx", "gy")
    return jax.shard_map(
        functools.partial(shards, mesh.shape["gy"]), mesh=mesh,
        in_specs=(spec, P(), P()), out_specs=spec, check_vma=False)
```
